128 devices in a mesh: expert: 32 (over z, x, core), replica: 4 (over y).
Axes of the slice: x: 4, y: 4, z: 4, core: 2. Of those that a mesh axis runs over, the one named last changes fastest.
Arguments:
- grad_out: bfloat16 [16384, 2048], P(('expert', 'replica')), may hold values from -6 to 6
- gates: bfloat16 [16384, 8], P(('expert', 'replica')), may hold values from 0.019897461 to 0.5
- experts: int32 [16384, 8], P(('expert', 'replica')), may hold values from 0 to 127, all different within a row; in each aligned block of 128 rows (0 to 127, 128 to 255, ...) at most 20 rows name the same one
- hidden: bfloat16 [128, 4, 640, 768], P('expert', 'replica'), may hold values from -6 to 6
- down_weight: bfloat16 [2048, 128, 768], P(None, 'expert'), may hold values from -0.21875 to 0.21875
Outputs:
- d_hidden: bfloat16 [128, 4, 640, 768], P('expert', 'replica')
- d_down: bfloat16 [2048, 128, 768], P('replica', 'expert')
- d_gates: float32 [16384, 8], P(('expert', 'replica'))
The draws below stay inside these ranges and needn't reach their ends.
Inputs may be any that keep to these rules, and one draw needn't show every extreme that they name: Each token names 8 different experts. Among the 128 tokens of one device no expert is named by more than 20 tokens, a bound that some block reaches.
All inputs are finite; a program needn't handle non-finite values.
Results may differ from the reference program's by a relative error of at most 0.013.
Values may be sent and summed in bfloat16 or wider, within the bound.
A program may use at most 192 MiB of HBM per device.

```python
import math
import jax
import jax.numpy as jnp
import numpy as np
from jax import lax

D = 2048
FF = 768
TOP = 8
TOK_DEV = 128
EXPERTS = 128
CAP = 20
SLOTS = 640
TOKENS = 16384
N_REPLICA = 4


def steps_of(own_key, extent, cuts, low, top_value):
    def one(dim, parts):
        draws = jax.random.uniform(jax.random.fold_in(jax.random.fold_in(own_key, 6), dim), (parts,), jnp.float32, low / len(cuts), top_value / len(cuts))
        return jnp.repeat(jnp.exp(draws), extent[dim] // parts).reshape((-1,) + (1,) * (len(extent) - dim - 1))

    loudness = one(*cuts[0])
    for cut in cuts[1:]:
        loudness = loudness * one(*cut)
    return loudness


def assign_block(rng, own, number, rows, amount, top, reach, skew):
    sequence = jax.random.permutation(rng, amount)
    heavy_load, ordinary = shares(amount, rows * top, reach, skew, True), shares(amount, rows * top, reach, skew, False)
    places = jnp.arange(amount)

    def named(tallies, offset_by):
        used = int((tallies > 0).sum())
        fixed = max(1, used // 4)
        passed = fixed + (places - fixed + offset_by * (used - fixed)) % max(1, amount - fixed)
        return jnp.zeros((amount,), jnp.int32).at[sequence[jnp.where(places < fixed, places, passed)]].set(jnp.asarray(tallies, jnp.int32))

    tallies = jnp.where(number % 4 == 0, named(heavy_load, number // 4), named(ordinary, number - number // 4 - 1))
    mixed = jax.random.permutation(jax.random.fold_in(own, 3), amount)
    donor, taker = mixed[0:amount // 2 * 2:2], mixed[1:amount // 2 * 2:2]
    margin = jnp.minimum(tallies[donor] - 1, reach - tallies[taker]) // 2
    margin = jnp.where((donor == sequence[0]) | (taker == sequence[0]) | (tallies[taker] == 0), 0, jnp.maximum(margin, 0))
    passed = jax.random.randint(jax.random.fold_in(own, 4), (amount // 2,), 0, 1 << 20) % (margin + 1)
    tallies = tallies.at[donor].add(-passed).at[taker].add(passed)
    items = jnp.searchsorted(jnp.cumsum(tallies), jnp.arange(rows * top), side="right").astype(jnp.int32)
    grid = items.reshape(top, rows).T
    grid = grid[jax.random.permutation(jax.random.fold_in(own, 1), rows)]
    offset_by = jax.random.randint(jax.random.fold_in(own, 2), (rows, 1), 0, top)
    return jnp.take_along_axis(grid, (jnp.arange(top)[None, :] + offset_by) % top, axis=1)


def shares(amount, total, most, slope, full):
    weights = [(1 << 20) // math.isqrt(grade ** slope) + 1 for grade in range(1, amount + 1)]
    largest = most if full else min(most, max(-(-total // amount), total * weights[0] // sum(weights)))
    least = 1 if total - largest >= amount - 1 else 0
    holding, surplus = [largest] + [least] * (amount - 1), total - largest - least * (amount - 1)
    while surplus > 0:
        free = [i for i in range(1, amount) if holding[i] < largest] or [i for i in range(1, amount) if holding[i] < most]
        whole, left = sum([weights[i] for i in free]), surplus
        for i in free:
            extra = min(most - holding[i], max(1, left * weights[i] // whole), surplus)
            holding[i] = holding[i] + extra
            surplus = surplus - extra
    return np.array(holding)


def normal_values(stream_key, shape, width, reach, shards=(), kind=jnp.bfloat16):
    result = width * jax.random.normal(stream_key, shape, jnp.float32)
    if shards:
        result = result * steps_of(stream_key, shape, shards, -0.22, 0.18)
    return jnp.clip(result, -reach, reach).astype(kind)


def setup_inputs(seed: int = 0) -> dict:
    key_of = jax.random.split(jax.random.key(seed), 6)
    grad_out = normal_values(key_of[0], (TOKENS, D), 1.0, 6.0, ((0, 128),))
    gates = jnp.clip(jnp.exp(math.log(0.5) - 3.224016 * jax.random.uniform(key_of[1], (TOKENS, TOP), jnp.float32) ** steps_of(key_of[1], (TOKENS, TOP), ((0, 128),), -0.2, 0.2)), 0.019897461, 0.5).astype(jnp.bfloat16)
    experts_keys = jax.random.split(jax.random.fold_in(key_of[2], 1), TOKENS // TOK_DEV)
    experts_turns = jax.random.permutation(jax.random.fold_in(key_of[2], 3), TOKENS // TOK_DEV)
    experts = jax.vmap(lambda own, number: assign_block(jax.random.fold_in(key_of[2], 2), own, number, TOK_DEV, EXPERTS, TOP, CAP, 2))(experts_keys, experts_turns).reshape((TOKENS, TOP))
    hidden = normal_values(key_of[3], (EXPERTS, N_REPLICA, SLOTS, FF), 1.0, 6.0, ((0, 32), (1, 4)))
    down_weight = normal_values(key_of[4], (D, EXPERTS, FF), FF ** -0.5, 0.21875, ((1, 32),))
    return {"grad_out": grad_out, "gates": gates, "experts": experts, "hidden": hidden, "down_weight": down_weight}


def reference(grad_out, gates, experts, hidden, down_weight):
    block_count = TOKENS // TOK_DEV
    pairs = experts.reshape(block_count, TOK_DEV * TOP)
    expert_range = jnp.arange(EXPERTS, dtype=jnp.int32)
    onehot_ids = (pairs[:, :, None] == expert_range[None, None, :]).astype(jnp.int32)
    running = jnp.cumsum(onehot_ids, axis=1)
    position = (jnp.sum(onehot_ids * running, axis=2) - 1).reshape(TOKENS, TOP)
    token_ids = jnp.arange(TOKENS, dtype=jnp.int32)
    block_ids = token_ids // TOK_DEV
    source_ids = block_ids // N_REPLICA
    replica_ids = block_ids % N_REPLICA
    slot_index = (experts * N_REPLICA + replica_ids[:, None]) * SLOTS + source_ids[:, None] * CAP + position
    slot_flat = slot_index.reshape(-1).astype(jnp.int32)
    total_rows = EXPERTS * N_REPLICA * SLOTS
    owner_ids = jnp.full((total_rows,), TOKENS, jnp.int32)
    owner_ids = owner_ids.at[slot_flat].set(jnp.broadcast_to(token_ids[:, None], (TOKENS, TOP)).reshape(-1))
    slot_gates = jnp.zeros((total_rows,), jnp.float32).at[slot_flat].set(gates.astype(jnp.float32).reshape(-1))
    owner_ids = owner_ids.reshape(EXPERTS, N_REPLICA * SLOTS)
    slot_gates = slot_gates.reshape(EXPERTS, N_REPLICA * SLOTS)
    padded = jnp.concatenate([grad_out, jnp.zeros((1, D), jnp.bfloat16)], axis=0)
    weights_by_expert = jnp.moveaxis(down_weight, 1, 0)

    def one_expert(inputs):
        owner_rows, gate_row, held, weight_matrix = inputs
        grad_slots = jnp.take(padded, owner_rows, axis=0)
        upstream = jnp.dot(grad_slots, weight_matrix, preferred_element_type=jnp.float32)
        held_values = held.reshape(N_REPLICA * SLOTS, FF).astype(jnp.float32)
        hidden_grad = (gate_row[:, None] * upstream).astype(jnp.bfloat16)
        slot_grad = jnp.sum(held_values * upstream, axis=1)
        weighted = (gate_row[:, None] * held_values).astype(jnp.bfloat16)
        weighted = weighted.reshape(N_REPLICA, SLOTS, FF).astype(jnp.float32)
        grad_parts = grad_slots.reshape(N_REPLICA, SLOTS, D).astype(jnp.float32)
        partials = jnp.einsum("rsf,rsd->rdf", weighted, grad_parts)
        rounded = lax.optimization_barrier(partials.astype(jnp.bfloat16))
        down_grad = jnp.sum(rounded.astype(jnp.float32), axis=0).astype(jnp.bfloat16)
        return hidden_grad.reshape(N_REPLICA, SLOTS, FF), slot_grad, down_grad

    hidden_grad, slot_grad, down_grad = lax.map(one_expert, (owner_ids, slot_gates, hidden, weights_by_expert))
    d_down = jnp.transpose(down_grad, (1, 0, 2))
    d_gates = jnp.take(slot_grad.reshape(-1), slot_flat, axis=0).reshape(TOKENS, TOP)
    return hidden_grad, d_down, d_gates
```

```python
import jax
import jax.numpy as jnp
from jax import lax
from jax.sharding import PartitionSpec as P

N_CHUNKS = 4


def per_device(grad_out, gates, experts, hidden, down_weight):
    expert_count = lax.axis_size("expert")
    replica_count = lax.axis_size("replica")
    tok_rows = grad_out.shape[0]
    width = grad_out.shape[1]
    top_count = experts.shape[1]
    local_experts = hidden.shape[0]
    slot_count = hidden.shape[2]
    hidden_width = hidden.shape[3]
    capacity = slot_count // expert_count
    all_experts = local_experts * expert_count
    flat_ids = experts.reshape(-1)
    expert_range = jnp.arange(all_experts, dtype=jnp.int32)
    onehot_ids = (flat_ids[:, None] == expert_range[None, :]).astype(jnp.int32)
    running = jnp.cumsum(onehot_ids, axis=0)
    position = jnp.sum(onehot_ids * running, axis=1) - 1
    slot_index = (
        flat_ids % local_experts * expert_count + flat_ids // local_experts
    ) * capacity + position
    slot_index = slot_index.reshape(tok_rows, top_count)
    slot_range = jnp.arange(all_experts * capacity, dtype=jnp.int32)
    matches = slot_index[:, :, None] == slot_range[None, None, :]
    placing = jnp.any(matches, axis=1).astype(jnp.bfloat16)
    out_gates = jnp.sum(
        jnp.where(matches, gates[:, :, None].astype(jnp.float32), 0.0), axis=(0, 1)
    ).astype(jnp.bfloat16)
    out_gates = out_gates.reshape(local_experts, expert_count, capacity)
    gate_slots = lax.all_to_all(out_gates, "expert", split_axis=1, concat_axis=1, tiled=True)
    gate_slots = gate_slots.reshape(local_experts, slot_count).astype(jnp.float32)
    hidden_slots = hidden.reshape(local_experts, slot_count, hidden_width)
    weighted = (gate_slots[:, :, None] * hidden_slots.astype(jnp.float32)).astype(jnp.bfloat16)

    piece = width // (replica_count * N_CHUNKS)
    cols = grad_out.reshape(tok_rows, replica_count, N_CHUNKS, piece)
    rows = down_weight.reshape(replica_count, N_CHUNKS, piece, local_experts, hidden_width)
    upstream = None
    down_parts = []
    for c in range(N_CHUNKS):
        chunk = cols[:, :, c, :].reshape(tok_rows, replica_count * piece)
        outgoing = jnp.einsum(
            "tr,td->rd", placing, chunk, preferred_element_type=jnp.float32
        ).astype(jnp.bfloat16)
        outgoing = outgoing.reshape(local_experts, expert_count, capacity, replica_count * piece)
        grad_slots = lax.all_to_all(outgoing, "expert", split_axis=1, concat_axis=1, tiled=True)
        grad_slots = grad_slots.reshape(local_experts, slot_count, replica_count * piece)
        weight_rows = rows[:, c].reshape(replica_count * piece, local_experts, hidden_width)
        part = jnp.einsum(
            "esd,def->esf", grad_slots, weight_rows, preferred_element_type=jnp.float32
        )
        upstream = part if upstream is None else upstream + part
        down_parts.append(
            lax.psum_scatter(
                jnp.einsum(
                    "esd,esf->def", grad_slots, weighted, preferred_element_type=jnp.float32
                ).astype(jnp.bfloat16),
                "replica",
                scatter_dimension=0,
                tiled=True,
            )
        )
    down_grad = jnp.concatenate(down_parts, axis=0)
    hidden_grad = (gate_slots[:, :, None] * upstream).astype(jnp.bfloat16).reshape(hidden.shape)
    slot_grad = jnp.sum(hidden_slots.astype(jnp.float32) * upstream, axis=2)
    returned = lax.all_to_all(
        slot_grad.reshape(local_experts, expert_count, capacity),
        "expert",
        split_axis=1,
        concat_axis=1,
        tiled=True,
    )
    gate_grad = jnp.take(returned.reshape(-1), slot_index, axis=0)
    return (hidden_grad, down_grad, gate_grad)


def solution(mesh):
    in_specs = (
        P(("expert", "replica"), None),
        P(("expert", "replica"), None),
        P(("expert", "replica"), None),
        P("expert", "replica", None, None),
        P(None, "expert", None),
    )
    out_specs = (
        P("expert", "replica", None, None),
        P("replica", "expert", None),
        P(("expert", "replica"), None),
    )
    return jax.shard_map(
        per_device, mesh=mesh, in_specs=in_specs, out_specs=out_specs, check_vma=False
    )
```

```python
import functools

import jax
import jax.numpy as jnp
from jax import lax
from jax.experimental import pallas as pl
from jax.experimental.pallas import tpu as pltpu
from jax.sharding import PartitionSpec as P

N_CHUNKS = 4
MESH = pl.DeviceIdType.MESH


def exchange_kernel(n, out_ref, recv_ref, send_sems, recv_sems, local_sem):
    me = lax.axis_index("expert")
    rep = lax.axis_index("replica")
    barrier = pltpu.get_barrier_semaphore()

    def greet(k, carry):
        peer = lax.rem(me + k, n)
        pl.semaphore_signal(barrier, inc=1, device_id=(peer, rep), device_id_type=MESH)
        return carry

    lax.fori_loop(1, n, greet, 0)
    pl.semaphore_wait(barrier, n - 1)
    local = pltpu.make_async_copy(out_ref.at[me], recv_ref.at[me], local_sem)
    local.start()

    def send(k, carry):
        peer = lax.rem(me + k, n)
        pltpu.make_async_remote_copy(
            src_ref=out_ref.at[peer],
            dst_ref=recv_ref.at[me],
            send_sem=send_sems.at[peer],
            recv_sem=recv_sems.at[me],
            device_id=(peer, rep),
            device_id_type=MESH,
        ).start()
        return carry

    lax.fori_loop(1, n, send, 0)

    def finish(k, carry):
        peer = lax.rem(me + k, n)
        source = lax.rem(me + n - k, n)
        pltpu.make_async_remote_copy(
            src_ref=out_ref.at[peer],
            dst_ref=recv_ref.at[me],
            send_sem=send_sems.at[peer],
            recv_sem=recv_sems.at[me],
            device_id=(peer, rep),
            device_id_type=MESH,
        ).wait_send()
        pltpu.make_async_remote_copy(
            src_ref=out_ref.at[source],
            dst_ref=recv_ref.at[source],
            send_sem=send_sems.at[source],
            recv_sem=recv_sems.at[source],
            device_id=(source, rep),
            device_id_type=MESH,
        ).wait_recv()
        return carry

    lax.fori_loop(1, n, finish, 0)
    local.wait()


def exchange(outgoing, call_id):
    n = outgoing.shape[0]
    return pl.pallas_call(
        functools.partial(exchange_kernel, n),
        out_shape=jax.ShapeDtypeStruct(outgoing.shape, outgoing.dtype),
        in_specs=[pl.BlockSpec(memory_space=pl.ANY)],
        out_specs=pl.BlockSpec(memory_space=pl.ANY),
        scratch_shapes=[
            pltpu.SemaphoreType.DMA((n,)),
            pltpu.SemaphoreType.DMA((n,)),
            pltpu.SemaphoreType.DMA(()),
        ],
        compiler_params=pltpu.CompilerParams(collective_id=call_id, has_side_effects=True),
    )(outgoing)


def per_device(grad_out, gates, experts, hidden, down_weight):
    expert_count = lax.axis_size("expert")
    replica_count = lax.axis_size("replica")
    tok_rows = grad_out.shape[0]
    width = grad_out.shape[1]
    top_count = experts.shape[1]
    local_experts = hidden.shape[0]
    slot_count = hidden.shape[2]
    hidden_width = hidden.shape[3]
    capacity = slot_count // expert_count
    all_experts = local_experts * expert_count
    flat_ids = experts.reshape(-1)
    expert_range = jnp.arange(all_experts, dtype=jnp.int32)
    onehot_ids = (flat_ids[:, None] == expert_range[None, :]).astype(jnp.int32)
    running = jnp.cumsum(onehot_ids, axis=0)
    position = jnp.sum(onehot_ids * running, axis=1) - 1
    slot_index = (
        flat_ids % local_experts * expert_count + flat_ids // local_experts
    ) * capacity + position
    slot_index = slot_index.reshape(tok_rows, top_count)
    slot_range = jnp.arange(all_experts * capacity, dtype=jnp.int32)
    matches = slot_index[:, :, None] == slot_range[None, None, :]
    send_index = (flat_ids * capacity + position).reshape(tok_rows, top_count)
    placing = jnp.any(
        send_index[:, :, None] == slot_range[None, None, :], axis=1
    ).astype(jnp.bfloat16)
    out_gates = jnp.sum(
        jnp.where(matches, gates[:, :, None].astype(jnp.float32), 0.0), axis=(0, 1)
    ).astype(jnp.bfloat16)
    out_gates = out_gates.reshape(local_experts, expert_count, capacity)
    gate_slots = lax.all_to_all(out_gates, "expert", split_axis=1, concat_axis=1, tiled=True)
    gate_slots = gate_slots.reshape(local_experts, slot_count).astype(jnp.float32)
    hidden_slots = hidden.reshape(local_experts, slot_count, hidden_width)
    weighted = (gate_slots[:, :, None] * hidden_slots.astype(jnp.float32)).astype(jnp.bfloat16)

    piece = width // (replica_count * N_CHUNKS)
    cols = grad_out.reshape(tok_rows, replica_count, N_CHUNKS, piece)
    rows = down_weight.reshape(replica_count, N_CHUNKS, piece, local_experts, hidden_width)
    upstream = None
    down_parts = []
    for c in range(N_CHUNKS):
        chunk = cols[:, :, c, :].reshape(tok_rows, replica_count * piece)
        outgoing = jnp.einsum(
            "tr,td->rd", placing, chunk, preferred_element_type=jnp.float32
        ).astype(jnp.bfloat16)
        outgoing = outgoing.reshape(expert_count, local_experts * capacity, replica_count * piece)
        arrived = exchange(outgoing, c)
        grad_slots = arrived.reshape(expert_count, local_experts, capacity, replica_count * piece)
        grad_slots = jnp.transpose(grad_slots, (1, 0, 2, 3)).reshape(
            local_experts, slot_count, replica_count * piece
        )
        weight_rows = rows[:, c].reshape(replica_count * piece, local_experts, hidden_width)
        part = jnp.einsum(
            "esd,def->esf", grad_slots, weight_rows, preferred_element_type=jnp.float32
        )
        upstream = part if upstream is None else upstream + part
        down_parts.append(
            lax.psum_scatter(
                jnp.einsum(
                    "esd,esf->def", grad_slots, weighted, preferred_element_type=jnp.float32
                ).astype(jnp.bfloat16),
                "replica",
                scatter_dimension=0,
                tiled=True,
            )
        )
    down_grad = jnp.concatenate(down_parts, axis=0)
    hidden_grad = (gate_slots[:, :, None] * upstream).astype(jnp.bfloat16).reshape(hidden.shape)
    slot_grad = jnp.sum(hidden_slots.astype(jnp.float32) * upstream, axis=2)
    returned = lax.all_to_all(
        slot_grad.reshape(local_experts, expert_count, capacity),
        "expert",
        split_axis=1,
        concat_axis=1,
        tiled=True,
    )
    gate_grad = jnp.take(returned.reshape(-1), slot_index, axis=0)
    return (hidden_grad, down_grad, gate_grad)


def solution(mesh):
    in_specs = (
        P(("expert", "replica"), None),
        P(("expert", "replica"), None),
        P(("expert", "replica"), None),
        P("expert", "replica", None, None),
        P(None, "expert", None),
    )
    out_specs = (
        P("expert", "replica", None, None),
        P("replica", "expert", None),
        P(("expert", "replica"), None),
    )
    return jax.shard_map(
        per_device, mesh=mesh, in_specs=in_specs, out_specs=out_specs, check_vma=False
    )
```

```python
import jax
import jax.numpy as jnp
from jax import lax
from jax.sharding import PartitionSpec as P

N_CHUNKS = 4


def per_device(grad_out, gates, experts, hidden, down_weight):
    expert_count = lax.axis_size("expert")
    replica_count = lax.axis_size("replica")
    me = lax.axis_index("expert")
    tok_rows = grad_out.shape[0]
    width = grad_out.shape[1]
    top_count = experts.shape[1]
    local_experts = hidden.shape[0]
    slot_count = hidden.shape[2]
    hidden_width = hidden.shape[3]
    capacity = slot_count // expert_count
    all_experts = local_experts * expert_count

    flat_ids = experts.reshape(-1)
    expert_range = jnp.arange(all_experts, dtype=jnp.int32)
    onehot_ids = (flat_ids[:, None] == expert_range[None, :]).astype(jnp.int32)
    running = jnp.cumsum(onehot_ids, axis=0)
    position = jnp.sum(onehot_ids * running, axis=1) - 1
    slot_index = (
        flat_ids % local_experts * expert_count + flat_ids // local_experts
    ) * capacity + position
    slot_index = slot_index.reshape(tok_rows, top_count)

    info = jnp.concatenate([experts.astype(jnp.float32), gates.astype(jnp.float32)], axis=1)
    all_info = lax.all_gather(info, "expert")
    all_ids = all_info[:, :, :top_count].astype(jnp.int32).reshape(expert_count, tok_rows * top_count)
    all_gates = all_info[:, :, top_count:]
    local_ids = all_ids - me * local_experts
    mine = local_ids[:, :, None] == jnp.arange(local_experts, dtype=jnp.int32)[None, None, :]
    rank = jnp.cumsum(mine.astype(jnp.int32), axis=1) - 1
    rank = jnp.where(mine, rank, -1)
    owns = rank[..., None] == jnp.arange(capacity, dtype=jnp.int32)
    owns = owns.reshape(expert_count, tok_rows, top_count, local_experts, capacity)
    select = jnp.any(owns, axis=2).astype(jnp.bfloat16)
    gate_slots = jnp.sum(
        jnp.where(owns, all_gates[:, :, :, None, None], 0.0), axis=(1, 2)
    )
    gate_slots = jnp.transpose(gate_slots, (1, 0, 2)).reshape(local_experts, slot_count)

    gathered = lax.all_gather(grad_out, "expert")
    grad_slots = jnp.einsum(
        "stjp,std->jspd", select, gathered, preferred_element_type=jnp.float32
    ).astype(jnp.bfloat16).reshape(local_experts, slot_count, width)

    hidden_slots = hidden.reshape(local_experts, slot_count, hidden_width)
    weighted = (gate_slots[:, :, None] * hidden_slots.astype(jnp.float32)).astype(jnp.bfloat16)

    piece = width // (replica_count * N_CHUNKS)
    parts = grad_slots.reshape(local_experts, slot_count, replica_count, N_CHUNKS, piece)
    down_parts = []
    for c in range(N_CHUNKS):
        chunk = parts[:, :, :, c, :].reshape(local_experts, slot_count, replica_count * piece)
        down_parts.append(
            lax.psum_scatter(
                jnp.einsum(
                    "esd,esf->def", chunk, weighted, preferred_element_type=jnp.float32
                ).astype(jnp.bfloat16),
                "replica",
                scatter_dimension=0,
                tiled=True,
            )
        )
    down_grad = jnp.concatenate(down_parts, axis=0)
    upstream = jnp.einsum(
        "esd,def->esf", grad_slots, down_weight, preferred_element_type=jnp.float32
    )
    hidden_grad = (gate_slots[:, :, None] * upstream).astype(jnp.bfloat16).reshape(hidden.shape)
    slot_grad = jnp.sum(hidden_slots.astype(jnp.float32) * upstream, axis=2)
    returned = lax.all_to_all(
        slot_grad.reshape(local_experts, expert_count, capacity),
        "expert",
        split_axis=1,
        concat_axis=1,
        tiled=True,
    )
    gate_grad = jnp.take(returned.reshape(-1), slot_index, axis=0)
    return (hidden_grad, down_grad, gate_grad)


def solution(mesh):
    in_specs = (
        P(("expert", "replica"), None),
        P(("expert", "replica"), None),
        P(("expert", "replica"), None),
        P("expert", "replica", None, None),
        P(None, "expert", None),
    )
    out_specs = (
        P("expert", "replica", None, None),
        P("replica", "expert", None),
        P(("expert", "replica"), None),
    )
    return jax.shard_map(
        per_device, mesh=mesh, in_specs=in_specs, out_specs=out_specs, check_vma=False
    )
```

```python
import jax
import jax.numpy as jnp
from jax import lax
from jax.sharding import PartitionSpec as P

N_CHUNKS = 2


def per_device(grad_out, gates, experts, hidden, down_weight):
    expert_count = lax.axis_size("expert")
    replica_count = lax.axis_size("replica")
    me = lax.axis_index("expert")
    tok_rows = grad_out.shape[0]
    width = grad_out.shape[1]
    top_count = experts.shape[1]
    local_experts = hidden.shape[0]
    slot_count = hidden.shape[2]
    hidden_width = hidden.shape[3]
    capacity = slot_count // expert_count
    all_experts = local_experts * expert_count

    flat_ids = experts.reshape(-1)
    expert_range = jnp.arange(all_experts, dtype=jnp.int32)
    onehot_ids = (flat_ids[:, None] == expert_range[None, :]).astype(jnp.int32)
    running = jnp.cumsum(onehot_ids, axis=0)
    position = jnp.sum(onehot_ids * running, axis=1) - 1
    slot_index = (
        flat_ids % local_experts * expert_count + flat_ids // local_experts
    ) * capacity + position
    slot_index = slot_index.reshape(tok_rows, top_count)

    extra = 128
    info = jnp.concatenate(
        [
            grad_out,
            experts.astype(jnp.bfloat16),
            gates,
            jnp.zeros((tok_rows, extra - 2 * top_count), jnp.bfloat16),
        ],
        axis=1,
    )
    gathered = lax.all_gather(info, "expert")
    all_ids = gathered[:, :, width:width + top_count].astype(jnp.int32)
    all_gates = gathered[:, :, width + top_count:width + 2 * top_count].astype(jnp.float32)
    pair_ids = all_ids.reshape(expert_count, tok_rows * top_count).T
    local_ids = pair_ids - me * local_experts
    mine = local_ids[:, :, None] == jnp.arange(local_experts, dtype=jnp.int32)[None, None, :]
    mine = mine.reshape(tok_rows * top_count, expert_count * local_experts).astype(jnp.int32)
    rank = jnp.cumsum(mine, axis=0) - 1
    rank = jnp.where(mine > 0, rank, -1).reshape(tok_rows, top_count, expert_count, local_experts)
    owns = rank[..., None] == jnp.arange(capacity, dtype=jnp.int32)
    select = jnp.any(owns, axis=1)
    select = jnp.transpose(select, (1, 2, 3, 0)).reshape(
        expert_count, local_experts * capacity, tok_rows
    ).astype(jnp.bfloat16)
    gate_t = jnp.transpose(all_gates, (1, 2, 0))
    gate_slots = jnp.sum(
        jnp.where(owns, gate_t[:, :, :, None, None], 0.0), axis=(0, 1)
    )
    gate_slots = jnp.transpose(gate_slots, (1, 0, 2)).reshape(local_experts, slot_count)

    picked = jnp.einsum(
        "sqt,std->sqd", select, gathered, preferred_element_type=jnp.float32
    ).astype(jnp.bfloat16)
    picked = picked.reshape(expert_count, local_experts, capacity, width + extra)[:, :, :, :width]
    grad_slots = jnp.transpose(picked, (1, 0, 2, 3)).reshape(local_experts, slot_count, width)

    hidden_slots = hidden.reshape(local_experts, slot_count, hidden_width)
    weighted = (gate_slots[:, :, None] * hidden_slots.astype(jnp.float32)).astype(jnp.bfloat16)

    piece = width // (replica_count * N_CHUNKS)
    parts = grad_slots.reshape(local_experts, slot_count, replica_count, N_CHUNKS, piece)
    down_parts = []
    for c in range(N_CHUNKS):
        chunk = parts[:, :, :, c, :].reshape(local_experts, slot_count, replica_count * piece)
        down_parts.append(
            lax.psum_scatter(
                jnp.einsum(
                    "esd,esf->def", chunk, weighted, preferred_element_type=jnp.float32
                ).astype(jnp.bfloat16),
                "replica",
                scatter_dimension=0,
                tiled=True,
            )
        )
    down_grad = jnp.concatenate(down_parts, axis=0)
    upstream = jnp.einsum(
        "esd,def->esf", grad_slots, down_weight, preferred_element_type=jnp.float32
    )
    hidden_grad = (gate_slots[:, :, None] * upstream).astype(jnp.bfloat16).reshape(hidden.shape)
    slot_grad = jnp.sum(hidden_slots.astype(jnp.float32) * upstream, axis=2)
    returned = lax.all_to_all(
        slot_grad.reshape(local_experts, expert_count, capacity),
        "expert",
        split_axis=1,
        concat_axis=1,
        tiled=True,
    )
    gate_grad = jnp.take(returned.reshape(-1), slot_index, axis=0)
    return (hidden_grad, down_grad, gate_grad)


def solution(mesh):
    in_specs = (
        P(("expert", "replica"), None),
        P(("expert", "replica"), None),
        P(("expert", "replica"), None),
        P("expert", "replica", None, None),
        P(None, "expert", None),
    )
    out_specs = (
        P("expert", "replica", None, None),
        P("replica", "expert", None),
        P(("expert", "replica"), None),
    )
    return jax.shard_map(
        per_device, mesh=mesh, in_specs=in_specs, out_specs=out_specs, check_vma=False
    )
```

```python
import jax
import jax.numpy as jnp
from jax import lax
from jax.sharding import PartitionSpec as P


def per_device(grad_out, gates, experts, hidden, down_weight):
    expert_count = lax.axis_size("expert")
    replica_count = lax.axis_size("replica")
    me = lax.axis_index("expert")
    tok_rows = grad_out.shape[0]
    width = grad_out.shape[1]
    top_count = experts.shape[1]
    local_experts = hidden.shape[0]
    slot_count = hidden.shape[2]
    hidden_width = hidden.shape[3]
    capacity = slot_count // expert_count
    all_experts = local_experts * expert_count

    flat_ids = experts.reshape(-1)
    expert_range = jnp.arange(all_experts, dtype=jnp.int32)
    onehot_ids = (flat_ids[:, None] == expert_range[None, :]).astype(jnp.int32)
    running = jnp.cumsum(onehot_ids, axis=0)
    position = jnp.sum(onehot_ids * running, axis=1) - 1
    slot_index = (
        flat_ids % local_experts * expert_count + flat_ids // local_experts
    ) * capacity + position
    slot_index = slot_index.reshape(tok_rows, top_count)

    extra = 128
    info = jnp.concatenate(
        [
            grad_out,
            experts.astype(jnp.bfloat16),
            gates,
            jnp.zeros((tok_rows, extra - 2 * top_count), jnp.bfloat16),
        ],
        axis=1,
    )
    gathered = lax.all_gather(info, "expert")
    all_ids = gathered[:, :, width:width + top_count].astype(jnp.int32)
    all_gates = gathered[:, :, width + top_count:width + 2 * top_count].astype(jnp.float32)
    pair_ids = all_ids.reshape(expert_count, tok_rows * top_count).T
    local_ids = pair_ids - me * local_experts
    mine = local_ids[:, :, None] == jnp.arange(local_experts, dtype=jnp.int32)[None, None, :]
    mine = mine.reshape(tok_rows * top_count, expert_count * local_experts).astype(jnp.int32)
    rank = jnp.cumsum(mine, axis=0) - 1
    rank = jnp.where(mine > 0, rank, -1).reshape(tok_rows, top_count, expert_count, local_experts)
    owns = rank[..., None] == jnp.arange(capacity, dtype=jnp.int32)
    select = jnp.any(owns, axis=1)
    gate_t = jnp.transpose(all_gates, (1, 2, 0))
    gate_slots = jnp.sum(
        jnp.where(owns, gate_t[:, :, :, None, None], 0.0), axis=(0, 1)
    )
    gate_slots = jnp.transpose(gate_slots, (1, 0, 2)).reshape(local_experts, slot_count)

    group = 4
    groups = expert_count // group
    select = jnp.transpose(select, (2, 1, 3, 0)).reshape(
        local_experts, groups, group, capacity, 1, tok_rows
    )
    diagonal = jnp.eye(group, dtype=jnp.bool_).reshape(1, 1, group, 1, group, 1)
    blocks = jnp.logical_and(select, diagonal).astype(jnp.bfloat16).reshape(
        local_experts, groups, group * capacity, group * tok_rows
    )
    rows_of = gathered[:, :, :width].reshape(groups, group * tok_rows, width)
    grad_slots = jnp.einsum(
        "jgqu,gud->jgqd", blocks, rows_of, preferred_element_type=jnp.float32
    ).astype(jnp.bfloat16).reshape(local_experts, slot_count, width)

    hidden_slots = hidden.reshape(local_experts, slot_count, hidden_width)
    weighted = (gate_slots[:, :, None] * hidden_slots.astype(jnp.float32)).astype(jnp.bfloat16)

    down_grad = lax.psum_scatter(
        jnp.einsum(
            "esd,esf->def", grad_slots, weighted, preferred_element_type=jnp.float32
        ).astype(jnp.bfloat16),
        "replica",
        scatter_dimension=0,
        tiled=True,
    )
    upstream = jnp.einsum(
        "esd,def->esf", grad_slots, down_weight, preferred_element_type=jnp.float32
    )
    hidden_grad = (gate_slots[:, :, None] * upstream).astype(jnp.bfloat16).reshape(hidden.shape)
    slot_grad = jnp.sum(hidden_slots.astype(jnp.float32) * upstream, axis=2)
    returned = lax.all_to_all(
        slot_grad.reshape(local_experts, expert_count, capacity),
        "expert",
        split_axis=1,
        concat_axis=1,
        tiled=True,
    )
    gate_grad = jnp.take(returned.reshape(-1), slot_index, axis=0)
    return (hidden_grad, down_grad, gate_grad)


def solution(mesh):
    in_specs = (
        P(("expert", "replica"), None),
        P(("expert", "replica"), None),
        P(("expert", "replica"), None),
        P("expert", "replica", None, None),
        P(None, "expert", None),
    )
    out_specs = (
        P("expert", "replica", None, None),
        P("replica", "expert", None),
        P(("expert", "replica"), None),
    )
    return jax.shard_map(
        per_device, mesh=mesh, in_specs=in_specs, out_specs=out_specs, check_vma=False
    )
```

```python
import jax
import jax.numpy as jnp
from jax import lax
from jax.experimental import pallas as pl
from jax.sharding import PartitionSpec as P


def pick_kernel(column_ref, rows_ref, out_ref):
    column = column_ref[0, 0]
    group, tok, width = rows_ref.shape
    onehot = (
        column == lax.broadcasted_iota(jnp.int32, (column.shape[0], group * tok), 1)
    ).astype(rows_ref.dtype)
    rows = rows_ref[...].reshape(group * tok, width)
    out_ref[0, 0] = jnp.dot(onehot, rows, preferred_element_type=jnp.float32).astype(
        out_ref.dtype
    )


def pick(column, gathered, width):
    local_experts, groups, block, _ = column.shape
    sources, tok, _ = gathered.shape
    group = sources // groups
    return pl.pallas_call(
        pick_kernel,
        out_shape=jax.ShapeDtypeStruct((local_experts, groups, block, width), gathered.dtype),
        grid=(groups, local_experts),
        in_specs=[
            pl.BlockSpec((1, 1, block, 1), lambda g, j: (j, g, 0, 0)),
            pl.BlockSpec((group, tok, width), lambda g, j: (g, 0, 0)),
        ],
        out_specs=pl.BlockSpec((1, 1, block, width), lambda g, j: (j, g, 0, 0)),
        cost_estimate=pl.CostEstimate(
            flops=2 * local_experts * groups * block * group * tok * width,
            bytes_accessed=sources * tok * width * 2 + local_experts * groups * block * width * 2,
            transcendentals=0,
        ),
    )(column, gathered)


def per_device(grad_out, gates, experts, hidden, down_weight):
    expert_count = lax.axis_size("expert")
    replica_count = lax.axis_size("replica")
    me = lax.axis_index("expert")
    tok_rows = grad_out.shape[0]
    width = grad_out.shape[1]
    top_count = experts.shape[1]
    local_experts = hidden.shape[0]
    slot_count = hidden.shape[2]
    hidden_width = hidden.shape[3]
    capacity = slot_count // expert_count
    all_experts = local_experts * expert_count

    flat_ids = experts.reshape(-1)
    expert_range = jnp.arange(all_experts, dtype=jnp.int32)
    onehot_ids = (flat_ids[:, None] == expert_range[None, :]).astype(jnp.int32)
    running = jnp.cumsum(onehot_ids, axis=0)
    position = jnp.sum(onehot_ids * running, axis=1) - 1
    slot_index = (
        flat_ids % local_experts * expert_count + flat_ids // local_experts
    ) * capacity + position
    slot_index = slot_index.reshape(tok_rows, top_count)

    extra = 128
    info = jnp.concatenate(
        [
            grad_out,
            experts.astype(jnp.bfloat16),
            gates,
            jnp.zeros((tok_rows, extra - 2 * top_count), jnp.bfloat16),
        ],
        axis=1,
    )
    gathered = lax.all_gather(info, "expert")
    all_ids = gathered[:, :, width:width + top_count].astype(jnp.int32)
    all_gates = gathered[:, :, width + top_count:width + 2 * top_count].astype(jnp.float32)
    pair_ids = all_ids.reshape(expert_count, tok_rows * top_count).T
    local_ids = pair_ids - me * local_experts
    mine = local_ids[:, :, None] == jnp.arange(local_experts, dtype=jnp.int32)[None, None, :]
    mine = mine.reshape(tok_rows * top_count, expert_count * local_experts).astype(jnp.int32)
    rank = jnp.cumsum(mine, axis=0) - 1
    rank = jnp.where(mine > 0, rank, -1).reshape(
        tok_rows * top_count, expert_count, local_experts
    )
    hit = rank[..., None] == jnp.arange(capacity, dtype=jnp.int32)
    token_of = (jnp.arange(tok_rows * top_count, dtype=jnp.int32) // top_count + 1)
    owner = jnp.sum(jnp.where(hit, token_of[:, None, None, None], 0), axis=0) - 1
    gate_pairs = all_gates.reshape(expert_count, tok_rows * top_count).T
    gate_slots = jnp.sum(jnp.where(hit, gate_pairs[:, :, None, None], 0.0), axis=0)
    gate_slots = jnp.transpose(gate_slots, (1, 0, 2)).reshape(local_experts, slot_count)

    group = 4
    groups = expert_count // group
    within = (jnp.arange(expert_count, dtype=jnp.int32) % group * tok_rows)[:, None, None]
    column = jnp.where(owner >= 0, owner + within, -1)
    column = jnp.transpose(column, (1, 0, 2)).reshape(
        local_experts, groups, group * capacity, 1
    )
    grad_slots = pick(column, gathered, width).reshape(local_experts, slot_count, width)

    hidden_slots = hidden.reshape(local_experts, slot_count, hidden_width)
    weighted = (gate_slots[:, :, None] * hidden_slots.astype(jnp.float32)).astype(jnp.bfloat16)

    down_grad = lax.psum_scatter(
        jnp.einsum(
            "esd,esf->def", grad_slots, weighted, preferred_element_type=jnp.float32
        ).astype(jnp.bfloat16),
        "replica",
        scatter_dimension=0,
        tiled=True,
    )
    upstream = jnp.einsum(
        "esd,def->esf", grad_slots, down_weight, preferred_element_type=jnp.float32
    )
    hidden_grad = (gate_slots[:, :, None] * upstream).astype(jnp.bfloat16).reshape(hidden.shape)
    slot_grad = jnp.sum(hidden_slots.astype(jnp.float32) * upstream, axis=2)
    returned = lax.all_to_all(
        slot_grad.reshape(local_experts, expert_count, capacity),
        "expert",
        split_axis=1,
        concat_axis=1,
        tiled=True,
    )
    gate_grad = jnp.take(returned.reshape(-1), slot_index, axis=0)
    return (hidden_grad, down_grad, gate_grad)


def solution(mesh):
    in_specs = (
        P(("expert", "replica"), None),
        P(("expert", "replica"), None),
        P(("expert", "replica"), None),
        P("expert", "replica", None, None),
        P(None, "expert", None),
    )
    out_specs = (
        P("expert", "replica", None, None),
        P("replica", "expert", None),
        P(("expert", "replica"), None),
    )
    return jax.shard_map(
        per_device, mesh=mesh, in_specs=in_specs, out_specs=out_specs, check_vma=False
    )
```

```python
import jax
import jax.numpy as jnp
from jax import lax
from jax.experimental import pallas as pl
from jax.sharding import PartitionSpec as P

N_CHUNKS = 2


def pick_kernel(column_ref, rows_ref, out_ref):
    column = column_ref[0]
    group, tok, width = out_ref.shape[0], rows_ref.shape[1], out_ref.shape[3]
    block = out_ref.shape[2]
    onehot = (
        column == lax.broadcasted_iota(jnp.int32, (column.shape[0], rows_ref.shape[0] * tok), 1)
    ).astype(rows_ref.dtype)
    rows = rows_ref[...].reshape(rows_ref.shape[0] * tok, width)
    result = jnp.dot(onehot, rows, preferred_element_type=jnp.float32).astype(out_ref.dtype)
    for j in range(group):
        out_ref[j, 0] = result[j * block:(j + 1) * block]


def pick(column, gathered, width, local):
    groups, rows_per, _ = column.shape
    sources, tok, _ = gathered.shape
    group = sources // groups
    block = rows_per // local
    return pl.pallas_call(
        pick_kernel,
        out_shape=jax.ShapeDtypeStruct((local, groups, block, width), gathered.dtype),
        grid=(groups,),
        in_specs=[
            pl.BlockSpec((1, rows_per, 1), lambda g: (g, 0, 0)),
            pl.BlockSpec((group, tok, width), lambda g: (g, 0, 0)),
        ],
        out_specs=pl.BlockSpec((local, 1, block, width), lambda g: (0, g, 0, 0)),
        cost_estimate=pl.CostEstimate(
            flops=2 * groups * rows_per * group * tok * width,
            bytes_accessed=sources * tok * width * 2 + groups * rows_per * width * 2,
            transcendentals=0,
        ),
    )(column, gathered)


def per_device(grad_out, gates, experts, hidden, down_weight):
    expert_count = lax.axis_size("expert")
    replica_count = lax.axis_size("replica")
    me = lax.axis_index("expert")
    tok_rows = grad_out.shape[0]
    width = grad_out.shape[1]
    top_count = experts.shape[1]
    local_experts = hidden.shape[0]
    slot_count = hidden.shape[2]
    hidden_width = hidden.shape[3]
    capacity = slot_count // expert_count
    all_experts = local_experts * expert_count

    flat_ids = experts.reshape(-1)
    expert_range = jnp.arange(all_experts, dtype=jnp.int32)
    onehot_ids = (flat_ids[:, None] == expert_range[None, :]).astype(jnp.int32)
    running = jnp.cumsum(onehot_ids, axis=0)
    position = jnp.sum(onehot_ids * running, axis=1) - 1
    slot_index = (
        flat_ids % local_experts * expert_count + flat_ids // local_experts
    ) * capacity + position
    slot_index = slot_index.reshape(tok_rows, top_count)

    piece = width // (replica_count * N_CHUNKS)
    chunk_width = replica_count * piece
    cols = grad_out.reshape(tok_rows, replica_count, N_CHUNKS, piece)
    extra = 128
    first = jnp.concatenate(
        [
            cols[:, :, 0, :].reshape(tok_rows, chunk_width),
            experts.astype(jnp.bfloat16),
            gates,
            jnp.zeros((tok_rows, extra - 2 * top_count), jnp.bfloat16),
        ],
        axis=1,
    )
    gathered = [lax.all_gather(first, "expert")]
    for c in range(1, N_CHUNKS):
        gathered.append(
            lax.all_gather(cols[:, :, c, :].reshape(tok_rows, chunk_width), "expert")
        )
    head = gathered[0]
    all_ids = head[:, :, chunk_width:chunk_width + top_count].astype(jnp.int32)
    all_gates = head[:, :, chunk_width + top_count:chunk_width + 2 * top_count].astype(
        jnp.float32
    )
    pair_ids = all_ids.reshape(expert_count, tok_rows * top_count).T
    local_ids = pair_ids - me * local_experts
    mine = local_ids[:, :, None] == jnp.arange(local_experts, dtype=jnp.int32)[None, None, :]
    mine = mine.reshape(tok_rows * top_count, expert_count * local_experts).astype(jnp.int32)
    rank = jnp.cumsum(mine, axis=0) - 1
    rank = jnp.where(mine > 0, rank, -1).reshape(
        tok_rows * top_count, expert_count, local_experts
    )
    hit = rank[..., None] == jnp.arange(capacity, dtype=jnp.int32)
    token_of = (jnp.arange(tok_rows * top_count, dtype=jnp.int32) // top_count + 1)
    owner = jnp.sum(jnp.where(hit, token_of[:, None, None, None], 0), axis=0) - 1
    gate_pairs = all_gates.reshape(expert_count, tok_rows * top_count).T
    gate_slots = jnp.sum(jnp.where(hit, gate_pairs[:, :, None, None], 0.0), axis=0)
    gate_slots = jnp.transpose(gate_slots, (1, 0, 2)).reshape(local_experts, slot_count)

    group = 4
    groups = expert_count // group
    within = (jnp.arange(expert_count, dtype=jnp.int32) % group * tok_rows)[:, None, None]
    column = jnp.where(owner >= 0, owner + within, -1)
    column = jnp.transpose(column.reshape(groups, group, local_experts, capacity), (0, 2, 1, 3))
    column = column.reshape(groups, local_experts * group * capacity, 1)
    slot_parts = [
        pick(column, part, chunk_width, local_experts).reshape(local_experts, slot_count, chunk_width)
        for part in gathered
    ]

    hidden_slots = hidden.reshape(local_experts, slot_count, hidden_width)
    weighted = (gate_slots[:, :, None] * hidden_slots.astype(jnp.float32)).astype(jnp.bfloat16)

    rows = down_weight.reshape(replica_count, N_CHUNKS, piece, local_experts, hidden_width)
    down_parts = []
    upstream = None
    for c, grad_slots in enumerate(slot_parts):
        down_parts.append(
            lax.psum_scatter(
                jnp.einsum(
                    "esd,esf->def", grad_slots, weighted, preferred_element_type=jnp.float32
                ).astype(jnp.bfloat16),
                "replica",
                scatter_dimension=0,
                tiled=True,
            )
        )
        weight_rows = rows[:, c].reshape(chunk_width, local_experts, hidden_width)
        part = jnp.einsum(
            "esd,def->esf", grad_slots, weight_rows, preferred_element_type=jnp.float32
        )
        upstream = part if upstream is None else upstream + part
    down_grad = jnp.concatenate(down_parts, axis=0)
    hidden_grad = (gate_slots[:, :, None] * upstream).astype(jnp.bfloat16).reshape(hidden.shape)
    slot_grad = jnp.sum(hidden_slots.astype(jnp.float32) * upstream, axis=2)
    returned = lax.all_to_all(
        slot_grad.reshape(local_experts, expert_count, capacity),
        "expert",
        split_axis=1,
        concat_axis=1,
        tiled=True,
    )
    gate_grad = jnp.take(returned.reshape(-1), slot_index, axis=0)
    return (hidden_grad, down_grad, gate_grad)


def solution(mesh):
    in_specs = (
        P(("expert", "replica"), None),
        P(("expert", "replica"), None),
        P(("expert", "replica"), None),
        P("expert", "replica", None, None),
        P(None, "expert", None),
    )
    out_specs = (
        P("expert", "replica", None, None),
        P("replica", "expert", None),
        P(("expert", "replica"), None),
    )
    return jax.shard_map(
        per_device, mesh=mesh, in_specs=in_specs, out_specs=out_specs, check_vma=False
    )
```

```python
import jax
import jax.numpy as jnp
from jax import lax
from jax.experimental import pallas as pl
from jax.sharding import PartitionSpec as P


def pick_kernel(column_ref, rows_ref, out_ref):
    column = column_ref[0]
    local, _, block, width = out_ref.shape
    group, tok, _ = rows_ref.shape
    onehot = (
        column == lax.broadcasted_iota(jnp.int32, (column.shape[0], group * tok), 1)
    ).astype(rows_ref.dtype)
    rows = rows_ref[...].reshape(group * tok, width)
    result = jnp.dot(onehot, rows, preferred_element_type=jnp.float32).astype(out_ref.dtype)
    for j in range(local):
        out_ref[j, 0] = result[j * block:(j + 1) * block]


def pick(column, gathered, width, local):
    groups, rows_per, _ = column.shape
    sources, tok, _ = gathered.shape
    group = sources // groups
    block = rows_per // local
    return pl.pallas_call(
        pick_kernel,
        out_shape=jax.ShapeDtypeStruct((local, groups, block, width), gathered.dtype),
        grid=(groups,),
        in_specs=[
            pl.BlockSpec((1, rows_per, 1), lambda g: (g, 0, 0)),
            pl.BlockSpec((group, tok, width), lambda g: (g, 0, 0)),
        ],
        out_specs=pl.BlockSpec((local, 1, block, width), lambda g: (0, g, 0, 0)),
        cost_estimate=pl.CostEstimate(
            flops=2 * groups * rows_per * group * tok * width,
            bytes_accessed=sources * tok * width * 2 + groups * rows_per * width * 2,
            transcendentals=0,
        ),
    )(column, gathered)


def per_device(grad_out, gates, experts, hidden, down_weight):
    expert_count = lax.axis_size("expert")
    replica_count = lax.axis_size("replica")
    me = lax.axis_index("expert")
    tok_rows = grad_out.shape[0]
    width = grad_out.shape[1]
    top_count = experts.shape[1]
    local_experts = hidden.shape[0]
    slot_count = hidden.shape[2]
    hidden_width = hidden.shape[3]
    capacity = slot_count // expert_count
    all_experts = local_experts * expert_count

    flat_ids = experts.reshape(-1)
    expert_range = jnp.arange(all_experts, dtype=jnp.int32)
    onehot_ids = (flat_ids[:, None] == expert_range[None, :]).astype(jnp.int32)
    running = jnp.cumsum(onehot_ids, axis=0)
    position = jnp.sum(onehot_ids * running, axis=1) - 1
    slot_index = (
        flat_ids % local_experts * expert_count + flat_ids // local_experts
    ) * capacity + position
    slot_index = slot_index.reshape(tok_rows, top_count)

    extra = 128
    info = jnp.concatenate(
        [
            grad_out,
            experts.astype(jnp.bfloat16),
            gates,
            jnp.zeros((tok_rows, extra - 2 * top_count), jnp.bfloat16),
        ],
        axis=1,
    )
    gathered = lax.all_gather(info, "expert")
    all_ids = gathered[:, :, width:width + top_count].astype(jnp.int32)
    all_gates = gathered[:, :, width + top_count:width + 2 * top_count].astype(jnp.float32)
    pair_ids = all_ids.reshape(expert_count, tok_rows * top_count).T
    local_ids = pair_ids - me * local_experts
    mine = local_ids[:, :, None] == jnp.arange(local_experts, dtype=jnp.int32)[None, None, :]
    mine = mine.reshape(tok_rows * top_count, expert_count * local_experts).astype(jnp.int32)
    rank = jnp.cumsum(mine, axis=0) - 1
    rank = jnp.where(mine > 0, rank, -1).reshape(
        tok_rows * top_count, expert_count, local_experts
    )
    hit = rank[..., None] == jnp.arange(capacity, dtype=jnp.int32)
    token_of = (jnp.arange(tok_rows * top_count, dtype=jnp.int32) // top_count + 1)
    owner = jnp.sum(jnp.where(hit, token_of[:, None, None, None], 0), axis=0) - 1
    gate_pairs = all_gates.reshape(expert_count, tok_rows * top_count).T
    gate_slots = jnp.sum(jnp.where(hit, gate_pairs[:, :, None, None], 0.0), axis=0)
    gate_slots = jnp.transpose(gate_slots, (1, 0, 2)).reshape(local_experts, slot_count)

    group = 4
    groups = expert_count // group
    within = (jnp.arange(expert_count, dtype=jnp.int32) % group * tok_rows)[:, None, None]
    column = jnp.where(owner >= 0, owner + within, -1)
    column = jnp.transpose(column.reshape(groups, group, local_experts, capacity), (0, 2, 1, 3))
    column = column.reshape(groups, local_experts * group * capacity, 1)
    grad_slots = pick(column, gathered, width, local_experts).reshape(
        local_experts, slot_count, width
    )

    hidden_slots = hidden.reshape(local_experts, slot_count, hidden_width)
    weighted = (gate_slots[:, :, None] * hidden_slots.astype(jnp.float32)).astype(jnp.bfloat16)

    down_grad = lax.psum_scatter(
        jnp.einsum(
            "esd,esf->def", grad_slots, weighted, preferred_element_type=jnp.float32
        ).astype(jnp.bfloat16),
        "replica",
        scatter_dimension=0,
        tiled=True,
    )
    upstream = jnp.einsum(
        "esd,def->esf", grad_slots, down_weight, preferred_element_type=jnp.float32
    )
    hidden_grad = (gate_slots[:, :, None] * upstream).astype(jnp.bfloat16).reshape(hidden.shape)
    slot_grad = jnp.sum(hidden_slots.astype(jnp.float32) * upstream, axis=2)
    returned = lax.all_to_all(
        slot_grad.reshape(local_experts, expert_count, capacity),
        "expert",
        split_axis=1,
        concat_axis=1,
        tiled=True,
    )
    gate_grad = jnp.take(returned.reshape(-1), slot_index, axis=0)
    return (hidden_grad, down_grad, gate_grad)


def solution(mesh):
    in_specs = (
        P(("expert", "replica"), None),
        P(("expert", "replica"), None),
        P(("expert", "replica"), None),
        P("expert", "replica", None, None),
        P(None, "expert", None),
    )
    out_specs = (
        P("expert", "replica", None, None),
        P("replica", "expert", None),
        P(("expert", "replica"), None),
    )
    return jax.shard_map(
        per_device, mesh=mesh, in_specs=in_specs, out_specs=out_specs, check_vma=False
    )
```

```python
import jax
import jax.numpy as jnp
from jax import lax
from jax.experimental import pallas as pl
from jax.sharding import PartitionSpec as P


def pick_kernel(column_ref, rows_ref, out_ref):
    column = column_ref[0]
    local, _, block, width = out_ref.shape
    group, tok, _ = rows_ref.shape
    onehot = (
        column == lax.broadcasted_iota(jnp.int32, (column.shape[0], group * tok), 1)
    ).astype(rows_ref.dtype)
    rows = rows_ref[...].reshape(group * tok, width)
    result = jnp.dot(onehot, rows, preferred_element_type=jnp.float32).astype(out_ref.dtype)
    for j in range(local):
        out_ref[j, 0] = result[j * block:(j + 1) * block]


def pick(column, gathered, width, local):
    groups, rows_per, _ = column.shape
    sources, tok, _ = gathered.shape
    group = sources // groups
    block = rows_per // local
    return pl.pallas_call(
        pick_kernel,
        out_shape=jax.ShapeDtypeStruct((local, groups, block, width), gathered.dtype),
        grid=(groups,),
        in_specs=[
            pl.BlockSpec((1, rows_per, 1), lambda g: (g, 0, 0)),
            pl.BlockSpec((group, tok, width), lambda g: (g, 0, 0)),
        ],
        out_specs=pl.BlockSpec((local, 1, block, width), lambda g: (0, g, 0, 0)),
        cost_estimate=pl.CostEstimate(
            flops=2 * groups * rows_per * group * tok * width,
            bytes_accessed=sources * tok * width * 2 + groups * rows_per * width * 2,
            transcendentals=0,
        ),
    )(column, gathered)


def per_device(grad_out, gates, experts, hidden, down_weight):
    expert_count = lax.axis_size("expert")
    replica_count = lax.axis_size("replica")
    me = lax.axis_index("expert")
    tok_rows = grad_out.shape[0]
    width = grad_out.shape[1]
    top_count = experts.shape[1]
    local_experts = hidden.shape[0]
    slot_count = hidden.shape[2]
    hidden_width = hidden.shape[3]
    capacity = slot_count // expert_count
    all_experts = local_experts * expert_count

    flat_ids = experts.reshape(-1)
    expert_range = jnp.arange(all_experts, dtype=jnp.int32)
    onehot_ids = (flat_ids[:, None] == expert_range[None, :]).astype(jnp.int32)
    running = jnp.cumsum(onehot_ids, axis=0)
    position = jnp.sum(onehot_ids * running, axis=1) - 1
    slot_index = (
        flat_ids % local_experts * expert_count + flat_ids // local_experts
    ) * capacity + position
    slot_index = slot_index.reshape(tok_rows, top_count)

    info = jnp.concatenate([experts.astype(jnp.float32), gates.astype(jnp.float32)], axis=1)
    info = jnp.broadcast_to(info.reshape(1, -1), (expert_count, tok_rows * 2 * top_count))
    info = lax.all_to_all(info, "expert", split_axis=0, concat_axis=0, tiled=True)
    info = info.reshape(expert_count, tok_rows, 2 * top_count)
    all_ids = info[:, :, :top_count].astype(jnp.int32)
    all_gates = info[:, :, top_count:]
    gathered = lax.all_gather(grad_out, "expert")
    pair_ids = all_ids.reshape(expert_count, tok_rows * top_count).T
    local_ids = pair_ids - me * local_experts
    mine = local_ids[:, :, None] == jnp.arange(local_experts, dtype=jnp.int32)[None, None, :]
    mine = mine.reshape(tok_rows * top_count, expert_count * local_experts).astype(jnp.int32)
    rank = jnp.cumsum(mine, axis=0) - 1
    rank = jnp.where(mine > 0, rank, -1).reshape(
        tok_rows * top_count, expert_count, local_experts
    )
    hit = rank[..., None] == jnp.arange(capacity, dtype=jnp.int32)
    token_of = (jnp.arange(tok_rows * top_count, dtype=jnp.int32) // top_count + 1)
    owner = jnp.sum(jnp.where(hit, token_of[:, None, None, None], 0), axis=0) - 1
    gate_pairs = all_gates.reshape(expert_count, tok_rows * top_count).T
    gate_slots = jnp.sum(jnp.where(hit, gate_pairs[:, :, None, None], 0.0), axis=0)
    gate_slots = jnp.transpose(gate_slots, (1, 0, 2)).reshape(local_experts, slot_count)

    group = 4
    groups = expert_count // group
    within = (jnp.arange(expert_count, dtype=jnp.int32) % group * tok_rows)[:, None, None]
    column = jnp.where(owner >= 0, owner + within, -1)
    column = jnp.transpose(column.reshape(groups, group, local_experts, capacity), (0, 2, 1, 3))
    column = column.reshape(groups, local_experts * group * capacity, 1)
    grad_slots = pick(column, gathered, width, local_experts).reshape(
        local_experts, slot_count, width
    )

    hidden_slots = hidden.reshape(local_experts, slot_count, hidden_width)
    weighted = (gate_slots[:, :, None] * hidden_slots.astype(jnp.float32)).astype(jnp.bfloat16)

    down_grad = lax.psum_scatter(
        jnp.einsum(
            "esd,esf->def", grad_slots, weighted, preferred_element_type=jnp.float32
        ).astype(jnp.bfloat16),
        "replica",
        scatter_dimension=0,
        tiled=True,
    )
    upstream = jnp.einsum(
        "esd,def->esf", grad_slots, down_weight, preferred_element_type=jnp.float32
    )
    hidden_grad = (gate_slots[:, :, None] * upstream).astype(jnp.bfloat16).reshape(hidden.shape)
    slot_grad = jnp.sum(hidden_slots.astype(jnp.float32) * upstream, axis=2)
    returned = lax.all_to_all(
        slot_grad.reshape(local_experts, expert_count, capacity),
        "expert",
        split_axis=1,
        concat_axis=1,
        tiled=True,
    )
    gate_grad = jnp.take(returned.reshape(-1), slot_index, axis=0)
    return (hidden_grad, down_grad, gate_grad)


def solution(mesh):
    in_specs = (
        P(("expert", "replica"), None),
        P(("expert", "replica"), None),
        P(("expert", "replica"), None),
        P("expert", "replica", None, None),
        P(None, "expert", None),
    )
    out_specs = (
        P("expert", "replica", None, None),
        P("replica", "expert", None),
        P(("expert", "replica"), None),
    )
    return jax.shard_map(
        per_device, mesh=mesh, in_specs=in_specs, out_specs=out_specs, check_vma=False
    )
```

```python
import jax
import jax.numpy as jnp
from jax import lax
from jax.experimental import pallas as pl
from jax.sharding import PartitionSpec as P


def pick_kernel(column_ref, rows_ref, out_ref):
    column = column_ref[0]
    local, _, block, width = out_ref.shape
    group, tok, _ = rows_ref.shape
    onehot = (
        column == lax.broadcasted_iota(jnp.int32, (column.shape[0], group * tok), 1)
    ).astype(rows_ref.dtype)
    rows = rows_ref[...].reshape(group * tok, width)
    result = jnp.dot(onehot, rows, preferred_element_type=jnp.float32).astype(out_ref.dtype)
    for j in range(local):
        out_ref[j, 0] = result[j * block:(j + 1) * block]


def pick(column, gathered, width, local):
    groups, rows_per, _ = column.shape
    sources, tok, _ = gathered.shape
    group = sources // groups
    block = rows_per // local
    return pl.pallas_call(
        pick_kernel,
        out_shape=jax.ShapeDtypeStruct((local, groups, block, width), gathered.dtype),
        grid=(groups,),
        in_specs=[
            pl.BlockSpec((1, rows_per, 1), lambda g: (g, 0, 0)),
            pl.BlockSpec((group, tok, width), lambda g: (g, 0, 0)),
        ],
        out_specs=pl.BlockSpec((local, 1, block, width), lambda g: (0, g, 0, 0)),
        cost_estimate=pl.CostEstimate(
            flops=2 * groups * rows_per * group * tok * width,
            bytes_accessed=sources * tok * width * 2 + groups * rows_per * width * 2,
            transcendentals=0,
        ),
    )(column, gathered)


def per_device(grad_out, gates, experts, hidden, down_weight):
    expert_count = lax.axis_size("expert")
    replica_count = lax.axis_size("replica")
    me = lax.axis_index("expert")
    tok_rows = grad_out.shape[0]
    width = grad_out.shape[1]
    top_count = experts.shape[1]
    local_experts = hidden.shape[0]
    slot_count = hidden.shape[2]
    hidden_width = hidden.shape[3]
    capacity = slot_count // expert_count
    all_experts = local_experts * expert_count

    flat_ids = experts.reshape(-1)
    expert_range = jnp.arange(all_experts, dtype=jnp.int32)
    onehot_ids = (flat_ids[:, None] == expert_range[None, :]).astype(jnp.int32)
    running = jnp.cumsum(onehot_ids, axis=0)
    position = jnp.sum(onehot_ids * running, axis=1) - 1
    slot_index = (
        flat_ids % local_experts * expert_count + flat_ids // local_experts
    ) * capacity + position
    slot_index = slot_index.reshape(tok_rows, top_count)

    info = jnp.concatenate([experts.astype(jnp.float32), gates.astype(jnp.float32)], axis=1)
    info = jnp.broadcast_to(info.reshape(1, -1), (expert_count, tok_rows * 2 * top_count))
    info = lax.all_to_all(info, "expert", split_axis=0, concat_axis=0, tiled=True)
    info = info.reshape(expert_count, tok_rows, 2 * top_count)
    all_ids = info[:, :, :top_count].astype(jnp.int32)
    all_gates = info[:, :, top_count:]
    gathered = lax.all_gather(grad_out, "expert")
    pair_ids = all_ids.reshape(expert_count, tok_rows * top_count).T
    local_ids = pair_ids - me * local_experts
    mine = local_ids[:, :, None] == jnp.arange(local_experts, dtype=jnp.int32)[None, None, :]
    mine = mine.reshape(tok_rows * top_count, expert_count * local_experts).astype(jnp.int32)
    rank = jnp.cumsum(mine, axis=0) - 1
    rank = jnp.where(mine > 0, rank, -1).reshape(
        tok_rows * top_count, expert_count, local_experts
    )
    hit = rank[..., None] == jnp.arange(capacity, dtype=jnp.int32)
    token_of = (jnp.arange(tok_rows * top_count, dtype=jnp.int32) // top_count + 1)
    owner = jnp.sum(jnp.where(hit, token_of[:, None, None, None], 0), axis=0) - 1
    gate_pairs = all_gates.reshape(expert_count, tok_rows * top_count).T
    gate_slots = jnp.sum(jnp.where(hit, gate_pairs[:, :, None, None], 0.0), axis=0)
    gate_slots = jnp.transpose(gate_slots, (1, 0, 2)).reshape(local_experts, slot_count)

    group = 4
    groups = expert_count // group
    within = (jnp.arange(expert_count, dtype=jnp.int32) % group * tok_rows)[:, None, None]
    column = jnp.where(owner >= 0, owner + within, -1)
    column = jnp.transpose(column.reshape(groups, group, local_experts, capacity), (0, 2, 1, 3))
    column = column.reshape(groups, local_experts * group * capacity, 1)
    grad_slots = pick(column, gathered, width, local_experts).reshape(
        local_experts, slot_count, width
    )

    hidden_slots = hidden.reshape(local_experts, slot_count, hidden_width)
    weighted = (gate_slots[:, :, None] * hidden_slots.astype(jnp.float32)).astype(jnp.bfloat16)

    down_grad = lax.psum_scatter(
        jnp.einsum(
            "esd,esf->edf", grad_slots, weighted, preferred_element_type=jnp.float32
        ).astype(jnp.bfloat16),
        "replica",
        scatter_dimension=1,
        tiled=True,
    )
    down_grad = jnp.transpose(down_grad, (1, 0, 2))
    upstream = jnp.einsum(
        "esd,def->esf", grad_slots, down_weight, preferred_element_type=jnp.float32
    )
    hidden_grad = (gate_slots[:, :, None] * upstream).astype(jnp.bfloat16).reshape(hidden.shape)
    slot_grad = jnp.sum(hidden_slots.astype(jnp.float32) * upstream, axis=2)
    returned = lax.all_to_all(
        slot_grad.reshape(local_experts, expert_count, capacity),
        "expert",
        split_axis=1,
        concat_axis=1,
        tiled=True,
    )
    gate_grad = jnp.take(returned.reshape(-1), slot_index, axis=0)
    return (hidden_grad, down_grad, gate_grad)


def solution(mesh):
    in_specs = (
        P(("expert", "replica"), None),
        P(("expert", "replica"), None),
        P(("expert", "replica"), None),
        P("expert", "replica", None, None),
        P(None, "expert", None),
    )
    out_specs = (
        P("expert", "replica", None, None),
        P("replica", "expert", None),
        P(("expert", "replica"), None),
    )
    return jax.shard_map(
        per_device, mesh=mesh, in_specs=in_specs, out_specs=out_specs, check_vma=False
    )
```

```python
import jax
import jax.numpy as jnp
from jax import lax
from jax.experimental import pallas as pl
from jax.sharding import PartitionSpec as P


def pick_kernel(column_ref, rows_ref, out_ref):
    column = column_ref[0]
    local, _, block, width = out_ref.shape
    group, tok, _ = rows_ref.shape
    onehot = (
        column == lax.broadcasted_iota(jnp.int32, (column.shape[0], group * tok), 1)
    ).astype(rows_ref.dtype)
    rows = rows_ref[...].reshape(group * tok, width)
    result = jnp.dot(onehot, rows, preferred_element_type=jnp.float32).astype(out_ref.dtype)
    for j in range(local):
        out_ref[j, 0] = result[j * block:(j + 1) * block]


def pick(column, gathered, width, local):
    groups, rows_per, _ = column.shape
    sources, tok, _ = gathered.shape
    group = sources // groups
    block = rows_per // local
    return pl.pallas_call(
        pick_kernel,
        out_shape=jax.ShapeDtypeStruct((local, groups, block, width), gathered.dtype),
        grid=(groups,),
        in_specs=[
            pl.BlockSpec((1, rows_per, 1), lambda g: (g, 0, 0)),
            pl.BlockSpec((group, tok, width), lambda g: (g, 0, 0)),
        ],
        out_specs=pl.BlockSpec((local, 1, block, width), lambda g: (0, g, 0, 0)),
        cost_estimate=pl.CostEstimate(
            flops=2 * groups * rows_per * group * tok * width,
            bytes_accessed=sources * tok * width * 2 + groups * rows_per * width * 2,
            transcendentals=0,
        ),
    )(column, gathered)


def per_device(grad_out, gates, experts, hidden, down_weight):
    expert_count = lax.axis_size("expert")
    replica_count = lax.axis_size("replica")
    me = lax.axis_index("expert")
    tok_rows = grad_out.shape[0]
    width = grad_out.shape[1]
    top_count = experts.shape[1]
    local_experts = hidden.shape[0]
    slot_count = hidden.shape[2]
    hidden_width = hidden.shape[3]
    capacity = slot_count // expert_count
    all_experts = local_experts * expert_count

    flat_ids = experts.reshape(-1)
    expert_range = jnp.arange(all_experts, dtype=jnp.int32)
    onehot_ids = (flat_ids[:, None] == expert_range[None, :]).astype(jnp.int32)
    running = jnp.cumsum(onehot_ids, axis=0)
    position = jnp.sum(onehot_ids * running, axis=1) - 1
    slot_index = (
        flat_ids % local_experts * expert_count + flat_ids // local_experts
    ) * capacity + position
    slot_index = slot_index.reshape(tok_rows, top_count)

    info = jnp.concatenate([experts.astype(jnp.float32), gates.astype(jnp.float32)], axis=1)
    info = jnp.broadcast_to(info.reshape(1, -1), (expert_count, tok_rows * 2 * top_count))
    info = lax.all_to_all(info, "expert", split_axis=0, concat_axis=0, tiled=True)
    info = info.reshape(expert_count, tok_rows, 2 * top_count)
    all_ids = info[:, :, :top_count].astype(jnp.int32)
    all_gates = info[:, :, top_count:]
    gathered = lax.all_gather(grad_out, "expert")
    pair_ids = all_ids.reshape(expert_count, tok_rows * top_count).T
    local_ids = pair_ids - me * local_experts
    mine = local_ids[:, :, None] == jnp.arange(local_experts, dtype=jnp.int32)[None, None, :]
    mine = mine.reshape(tok_rows * top_count, expert_count * local_experts).astype(jnp.int32)
    rank = jnp.cumsum(mine, axis=0) - 1
    rank = jnp.where(mine > 0, rank, -1).reshape(
        tok_rows * top_count, expert_count, local_experts
    )
    hit = rank[..., None] == jnp.arange(capacity, dtype=jnp.int32)
    token_of = (jnp.arange(tok_rows * top_count, dtype=jnp.int32) // top_count + 1)
    owner = jnp.sum(jnp.where(hit, token_of[:, None, None, None], 0), axis=0) - 1
    gate_pairs = all_gates.reshape(expert_count, tok_rows * top_count).T
    gate_slots = jnp.sum(jnp.where(hit, gate_pairs[:, :, None, None], 0.0), axis=0)
    gate_slots = jnp.transpose(gate_slots, (1, 0, 2)).reshape(local_experts, slot_count)

    group = 2
    groups = expert_count // group
    within = (jnp.arange(expert_count, dtype=jnp.int32) % group * tok_rows)[:, None, None]
    column = jnp.where(owner >= 0, owner + within, -1)
    column = jnp.transpose(column.reshape(groups, group, local_experts, capacity), (0, 2, 1, 3))
    column = column.reshape(groups, local_experts * group * capacity, 1)
    grad_slots = pick(column, gathered, width, local_experts).reshape(
        local_experts, slot_count, width
    )

    hidden_slots = hidden.reshape(local_experts, slot_count, hidden_width)
    weighted = (gate_slots[:, :, None] * hidden_slots.astype(jnp.float32)).astype(jnp.bfloat16)

    down_grad = lax.psum_scatter(
        jnp.einsum(
            "esd,esf->edf", grad_slots, weighted, preferred_element_type=jnp.float32
        ).astype(jnp.bfloat16),
        "replica",
        scatter_dimension=1,
        tiled=True,
    )
    down_grad = jnp.transpose(down_grad, (1, 0, 2))
    upstream = jnp.einsum(
        "esd,def->esf", grad_slots, down_weight, preferred_element_type=jnp.float32
    )
    hidden_grad = (gate_slots[:, :, None] * upstream).astype(jnp.bfloat16).reshape(hidden.shape)
    slot_grad = jnp.sum(hidden_slots.astype(jnp.float32) * upstream, axis=2)
    returned = lax.all_to_all(
        slot_grad.reshape(local_experts, expert_count, capacity),
        "expert",
        split_axis=1,
        concat_axis=1,
        tiled=True,
    )
    gate_grad = jnp.take(returned.reshape(-1), slot_index, axis=0)
    return (hidden_grad, down_grad, gate_grad)


def solution(mesh):
    in_specs = (
        P(("expert", "replica"), None),
        P(("expert", "replica"), None),
        P(("expert", "replica"), None),
        P("expert", "replica", None, None),
        P(None, "expert", None),
    )
    out_specs = (
        P("expert", "replica", None, None),
        P("replica", "expert", None),
        P(("expert", "replica"), None),
    )
    return jax.shard_map(
        per_device, mesh=mesh, in_specs=in_specs, out_specs=out_specs, check_vma=False
    )
```

```python
import jax
import jax.numpy as jnp
from jax import lax
from jax.experimental import pallas as pl
from jax.sharding import PartitionSpec as P


def pick_kernel(column_ref, mine_ref, theirs_ref, out_ref):
    column = column_ref[0]
    local, _, block, width = out_ref.shape
    pair, tok, _ = mine_ref.shape
    half = pair * tok
    onehot = (
        column == lax.broadcasted_iota(jnp.int32, (column.shape[0], 2 * half), 1)
    ).astype(mine_ref.dtype)
    result = jnp.dot(
        onehot[:, :half], mine_ref[...].reshape(half, width), preferred_element_type=jnp.float32
    ) + jnp.dot(
        onehot[:, half:], theirs_ref[...].reshape(half, width), preferred_element_type=jnp.float32
    )
    result = result.astype(out_ref.dtype)
    for j in range(local):
        out_ref[j, 0] = result[j * block:(j + 1) * block]


def pick(column, mine, theirs, local):
    groups, rows_per, _ = column.shape
    chips, tok, width = mine.shape
    pair = chips // groups
    block = rows_per // local
    spec = pl.BlockSpec((pair, tok, width), lambda g: (g, 0, 0))
    return pl.pallas_call(
        pick_kernel,
        out_shape=jax.ShapeDtypeStruct((local, groups, block, width), mine.dtype),
        grid=(groups,),
        in_specs=[pl.BlockSpec((1, rows_per, 1), lambda g: (g, 0, 0)), spec, spec],
        out_specs=pl.BlockSpec((local, 1, block, width), lambda g: (0, g, 0, 0)),
        cost_estimate=pl.CostEstimate(
            flops=4 * groups * rows_per * pair * tok * width,
            bytes_accessed=2 * chips * tok * width * 2 + groups * rows_per * width * 2,
            transcendentals=0,
        ),
    )(column, mine, theirs)


def per_device(grad_out, gates, experts, hidden, down_weight):
    expert_count = lax.axis_size("expert")
    replica_count = lax.axis_size("replica")
    me = lax.axis_index("expert")
    tok_rows = grad_out.shape[0]
    width = grad_out.shape[1]
    top_count = experts.shape[1]
    local_experts = hidden.shape[0]
    slot_count = hidden.shape[2]
    hidden_width = hidden.shape[3]
    capacity = slot_count // expert_count
    all_experts = local_experts * expert_count

    flat_ids = experts.reshape(-1)
    expert_range = jnp.arange(all_experts, dtype=jnp.int32)
    onehot_ids = (flat_ids[:, None] == expert_range[None, :]).astype(jnp.int32)
    running = jnp.cumsum(onehot_ids, axis=0)
    position = jnp.sum(onehot_ids * running, axis=1) - 1
    slot_index = (
        flat_ids % local_experts * expert_count + flat_ids // local_experts
    ) * capacity + position
    slot_index = slot_index.reshape(tok_rows, top_count)

    info = jnp.concatenate([experts.astype(jnp.float32), gates.astype(jnp.float32)], axis=1)
    info = jnp.broadcast_to(info.reshape(1, -1), (expert_count, tok_rows * 2 * top_count))
    info = lax.all_to_all(info, "expert", split_axis=0, concat_axis=0, tiled=True)
    info = info.reshape(expert_count, tok_rows, 2 * top_count)
    all_ids = info[:, :, :top_count].astype(jnp.int32)
    all_gates = info[:, :, top_count:]
    cores = 2
    core_groups = [list(range(c, expert_count, cores)) for c in range(cores)]
    mine_rows = lax.all_gather(grad_out, "expert", axis_index_groups=core_groups)
    theirs_rows = lax.ppermute(
        mine_rows, "expert", [(i, i ^ 1) for i in range(expert_count)]
    )
    pair_ids = all_ids.reshape(expert_count, tok_rows * top_count).T
    local_ids = pair_ids - me * local_experts
    mine = local_ids[:, :, None] == jnp.arange(local_experts, dtype=jnp.int32)[None, None, :]
    mine = mine.reshape(tok_rows * top_count, expert_count * local_experts).astype(jnp.int32)
    rank = jnp.cumsum(mine, axis=0) - 1
    rank = jnp.where(mine > 0, rank, -1).reshape(
        tok_rows * top_count, expert_count, local_experts
    )
    hit = rank[..., None] == jnp.arange(capacity, dtype=jnp.int32)
    token_of = (jnp.arange(tok_rows * top_count, dtype=jnp.int32) // top_count + 1)
    owner = jnp.sum(jnp.where(hit, token_of[:, None, None, None], 0), axis=0) - 1
    gate_pairs = all_gates.reshape(expert_count, tok_rows * top_count).T
    gate_slots = jnp.sum(jnp.where(hit, gate_pairs[:, :, None, None], 0.0), axis=0)
    gate_slots = jnp.transpose(gate_slots, (1, 0, 2)).reshape(local_experts, slot_count)

    group = 4
    groups = expert_count // group
    source = jnp.arange(expert_count, dtype=jnp.int32)
    other = (source % cores != me % cores).astype(jnp.int32)
    within = ((other * (group // cores) + source % group // cores) * tok_rows)[:, None, None]
    column = jnp.where(owner >= 0, owner + within, -1)
    column = jnp.transpose(column.reshape(groups, group, local_experts, capacity), (0, 2, 1, 3))
    column = column.reshape(groups, local_experts * group * capacity, 1)
    grad_slots = pick(column, mine_rows, theirs_rows, local_experts).reshape(
        local_experts, slot_count, width
    )

    hidden_slots = hidden.reshape(local_experts, slot_count, hidden_width)
    weighted = (gate_slots[:, :, None] * hidden_slots.astype(jnp.float32)).astype(jnp.bfloat16)

    down_grad = lax.psum_scatter(
        jnp.einsum(
            "esd,esf->def", grad_slots, weighted, preferred_element_type=jnp.float32
        ).astype(jnp.bfloat16),
        "replica",
        scatter_dimension=0,
        tiled=True,
    )
    upstream = jnp.einsum(
        "esd,def->esf", grad_slots, down_weight, preferred_element_type=jnp.float32
    )
    hidden_grad = (gate_slots[:, :, None] * upstream).astype(jnp.bfloat16).reshape(hidden.shape)
    slot_grad = jnp.sum(hidden_slots.astype(jnp.float32) * upstream, axis=2)
    returned = lax.all_to_all(
        slot_grad.reshape(local_experts, expert_count, capacity),
        "expert",
        split_axis=1,
        concat_axis=1,
        tiled=True,
    )
    gate_grad = jnp.take(returned.reshape(-1), slot_index, axis=0)
    return (hidden_grad, down_grad, gate_grad)


def solution(mesh):
    in_specs = (
        P(("expert", "replica"), None),
        P(("expert", "replica"), None),
        P(("expert", "replica"), None),
        P("expert", "replica", None, None),
        P(None, "expert", None),
    )
    out_specs = (
        P("expert", "replica", None, None),
        P("replica", "expert", None),
        P(("expert", "replica"), None),
    )
    return jax.shard_map(
        per_device, mesh=mesh, in_specs=in_specs, out_specs=out_specs, check_vma=False
    )
```

```python
import jax
import jax.numpy as jnp
from jax import lax
from jax.experimental import pallas as pl
from jax.sharding import PartitionSpec as P


def pick_kernel(column_ref, rows_ref, out_ref):
    column = column_ref[0]
    local, _, block, width = out_ref.shape
    group, tok, _ = rows_ref.shape
    onehot = (
        column == lax.broadcasted_iota(jnp.int32, (column.shape[0], group * tok), 1)
    ).astype(rows_ref.dtype)
    rows = rows_ref[...].reshape(group * tok, width)
    result = jnp.dot(onehot, rows, preferred_element_type=jnp.float32).astype(out_ref.dtype)
    for j in range(local):
        out_ref[j, 0] = result[j * block:(j + 1) * block]


def pick(column, gathered, width, local):
    groups, rows_per, _ = column.shape
    sources, tok, _ = gathered.shape
    group = sources // groups
    block = rows_per // local
    return pl.pallas_call(
        pick_kernel,
        out_shape=jax.ShapeDtypeStruct((local, groups, block, width), gathered.dtype),
        grid=(groups,),
        in_specs=[
            pl.BlockSpec((1, rows_per, 1), lambda g: (g, 0, 0)),
            pl.BlockSpec((group, tok, width), lambda g: (g, 0, 0)),
        ],
        out_specs=pl.BlockSpec((local, 1, block, width), lambda g: (0, g, 0, 0)),
        cost_estimate=pl.CostEstimate(
            flops=2 * groups * rows_per * group * tok * width,
            bytes_accessed=sources * tok * width * 2 + groups * rows_per * width * 2,
            transcendentals=0,
        ),
    )(column, gathered)


def per_device(grad_out, gates, experts, hidden, down_weight):
    expert_count = lax.axis_size("expert")
    replica_count = lax.axis_size("replica")
    me = lax.axis_index("expert")
    tok_rows = grad_out.shape[0]
    width = grad_out.shape[1]
    top_count = experts.shape[1]
    local_experts = hidden.shape[0]
    slot_count = hidden.shape[2]
    hidden_width = hidden.shape[3]
    capacity = slot_count // expert_count
    all_experts = local_experts * expert_count

    flat_ids = experts.reshape(-1)
    expert_range = jnp.arange(all_experts, dtype=jnp.int32)
    onehot_ids = (flat_ids[:, None] == expert_range[None, :]).astype(jnp.int32)
    running = jnp.cumsum(onehot_ids, axis=0)
    position = jnp.sum(onehot_ids * running, axis=1) - 1
    slot_index = (
        flat_ids % local_experts * expert_count + flat_ids // local_experts
    ) * capacity + position
    slot_index = slot_index.reshape(tok_rows, top_count)

    info = jnp.concatenate([experts.astype(jnp.float32), gates.astype(jnp.float32)], axis=1)
    info = jnp.broadcast_to(info.reshape(1, -1), (expert_count, tok_rows * 2 * top_count))
    info = lax.all_to_all(info, "expert", split_axis=0, concat_axis=0, tiled=True)
    info = info.reshape(expert_count, tok_rows, 2 * top_count)
    all_ids = info[:, :, :top_count].astype(jnp.int32)
    all_gates = info[:, :, top_count:]
    gathered = lax.all_gather(grad_out, "expert")
    pair_ids = all_ids.reshape(expert_count, tok_rows * top_count).T
    local_ids = pair_ids - me * local_experts
    mine = local_ids[:, :, None] == jnp.arange(local_experts, dtype=jnp.int32)[None, None, :]
    mine = mine.reshape(tok_rows * top_count, expert_count * local_experts).astype(jnp.int32)
    rank = jnp.cumsum(mine, axis=0) - 1
    rank = jnp.where(mine > 0, rank, -1).reshape(
        tok_rows * top_count, expert_count, local_experts
    )
    hit = rank[..., None] == jnp.arange(capacity, dtype=jnp.int32)
    token_of = (jnp.arange(tok_rows * top_count, dtype=jnp.int32) // top_count + 1)
    owner = jnp.sum(jnp.where(hit, token_of[:, None, None, None], 0), axis=0) - 1
    gate_pairs = all_gates.reshape(expert_count, tok_rows * top_count).T
    gate_slots = jnp.sum(jnp.where(hit, gate_pairs[:, :, None, None], 0.0), axis=0)
    gate_slots = jnp.transpose(gate_slots, (1, 0, 2)).reshape(local_experts, slot_count)

    group = 8
    groups = expert_count // group
    within = (jnp.arange(expert_count, dtype=jnp.int32) % group * tok_rows)[:, None, None]
    column = jnp.where(owner >= 0, owner + within, -1)
    column = jnp.transpose(column.reshape(groups, group, local_experts, capacity), (0, 2, 1, 3))
    column = column.reshape(groups, local_experts * group * capacity, 1)
    grad_slots = pick(column, gathered, width, local_experts).reshape(
        local_experts, slot_count, width
    )

    hidden_slots = hidden.reshape(local_experts, slot_count, hidden_width)
    weighted = (gate_slots[:, :, None] * hidden_slots.astype(jnp.float32)).astype(jnp.bfloat16)

    down_grad = lax.psum_scatter(
        jnp.einsum(
            "esd,esf->def", grad_slots, weighted, preferred_element_type=jnp.float32
        ).astype(jnp.bfloat16),
        "replica",
        scatter_dimension=0,
        tiled=True,
    )
    upstream = jnp.einsum(
        "esd,def->esf", grad_slots, down_weight, preferred_element_type=jnp.float32
    )
    hidden_grad = (gate_slots[:, :, None] * upstream).astype(jnp.bfloat16).reshape(hidden.shape)
    slot_grad = jnp.sum(hidden_slots.astype(jnp.float32) * upstream, axis=2)
    returned = lax.all_to_all(
        slot_grad.reshape(local_experts, expert_count, capacity),
        "expert",
        split_axis=1,
        concat_axis=1,
        tiled=True,
    )
    gate_grad = jnp.take(returned.reshape(-1), slot_index, axis=0)
    return (hidden_grad, down_grad, gate_grad)


def solution(mesh):
    in_specs = (
        P(("expert", "replica"), None),
        P(("expert", "replica"), None),
        P(("expert", "replica"), None),
        P("expert", "replica", None, None),
        P(None, "expert", None),
    )
    out_specs = (
        P("expert", "replica", None, None),
        P("replica", "expert", None),
        P(("expert", "replica"), None),
    )
    return jax.shard_map(
        per_device, mesh=mesh, in_specs=in_specs, out_specs=out_specs, check_vma=False
    )
```

```python
import jax
import jax.numpy as jnp
from jax import lax
from jax.experimental import pallas as pl
from jax.sharding import PartitionSpec as P


def pick_kernel(column_ref, rows_ref, out_ref):
    column = column_ref[0]
    local, _, block, width = out_ref.shape
    group, tok, _ = rows_ref.shape
    onehot = (
        column == lax.broadcasted_iota(jnp.int32, (column.shape[0], group * tok), 1)
    ).astype(rows_ref.dtype)
    rows = rows_ref[...].reshape(group * tok, width)
    result = jnp.dot(onehot, rows, preferred_element_type=jnp.float32).astype(out_ref.dtype)
    for j in range(local):
        out_ref[j, 0] = result[j * block:(j + 1) * block]


def pick(column, gathered, width, local):
    groups, rows_per, _ = column.shape
    sources, tok, _ = gathered.shape
    group = sources // groups
    block = rows_per // local
    span = 512
    return pl.pallas_call(
        pick_kernel,
        out_shape=jax.ShapeDtypeStruct((local, groups, block, width), gathered.dtype),
        grid=(groups, width // span),
        in_specs=[
            pl.BlockSpec((1, rows_per, 1), lambda g, n: (g, 0, 0)),
            pl.BlockSpec((group, tok, span), lambda g, n: (g, 0, n)),
        ],
        out_specs=pl.BlockSpec((local, 1, block, span), lambda g, n: (0, g, 0, n)),
        cost_estimate=pl.CostEstimate(
            flops=2 * groups * rows_per * group * tok * width,
            bytes_accessed=sources * tok * width * 2 + groups * rows_per * width * 2,
            transcendentals=0,
        ),
    )(column, gathered)


def per_device(grad_out, gates, experts, hidden, down_weight):
    expert_count = lax.axis_size("expert")
    replica_count = lax.axis_size("replica")
    me = lax.axis_index("expert")
    tok_rows = grad_out.shape[0]
    width = grad_out.shape[1]
    top_count = experts.shape[1]
    local_experts = hidden.shape[0]
    slot_count = hidden.shape[2]
    hidden_width = hidden.shape[3]
    capacity = slot_count // expert_count
    all_experts = local_experts * expert_count

    flat_ids = experts.reshape(-1)
    expert_range = jnp.arange(all_experts, dtype=jnp.int32)
    onehot_ids = (flat_ids[:, None] == expert_range[None, :]).astype(jnp.int32)
    running = jnp.cumsum(onehot_ids, axis=0)
    position = jnp.sum(onehot_ids * running, axis=1) - 1
    slot_index = (
        flat_ids % local_experts * expert_count + flat_ids // local_experts
    ) * capacity + position
    slot_index = slot_index.reshape(tok_rows, top_count)

    info = jnp.concatenate([experts.astype(jnp.float32), gates.astype(jnp.float32)], axis=1)
    info = jnp.broadcast_to(info.reshape(1, -1), (expert_count, tok_rows * 2 * top_count))
    info = lax.all_to_all(info, "expert", split_axis=0, concat_axis=0, tiled=True)
    info = info.reshape(expert_count, tok_rows, 2 * top_count)
    all_ids = info[:, :, :top_count].astype(jnp.int32)
    all_gates = info[:, :, top_count:]
    gathered = lax.all_gather(grad_out, "expert")
    pair_ids = all_ids.reshape(expert_count, tok_rows * top_count).T
    local_ids = pair_ids - me * local_experts
    mine = local_ids[:, :, None] == jnp.arange(local_experts, dtype=jnp.int32)[None, None, :]
    mine = mine.reshape(tok_rows * top_count, expert_count * local_experts).astype(jnp.int32)
    rank = jnp.cumsum(mine, axis=0) - 1
    rank = jnp.where(mine > 0, rank, -1).reshape(
        tok_rows * top_count, expert_count, local_experts
    )
    hit = rank[..., None] == jnp.arange(capacity, dtype=jnp.int32)
    token_of = (jnp.arange(tok_rows * top_count, dtype=jnp.int32) // top_count + 1)
    owner = jnp.sum(jnp.where(hit, token_of[:, None, None, None], 0), axis=0) - 1
    gate_pairs = all_gates.reshape(expert_count, tok_rows * top_count).T
    gate_slots = jnp.sum(jnp.where(hit, gate_pairs[:, :, None, None], 0.0), axis=0)
    gate_slots = jnp.transpose(gate_slots, (1, 0, 2)).reshape(local_experts, slot_count)

    group = 4
    groups = expert_count // group
    within = (jnp.arange(expert_count, dtype=jnp.int32) % group * tok_rows)[:, None, None]
    column = jnp.where(owner >= 0, owner + within, -1)
    column = jnp.transpose(column.reshape(groups, group, local_experts, capacity), (0, 2, 1, 3))
    column = column.reshape(groups, local_experts * group * capacity, 1)
    grad_slots = pick(column, gathered, width, local_experts).reshape(
        local_experts, slot_count, width
    )

    hidden_slots = hidden.reshape(local_experts, slot_count, hidden_width)
    weighted = (gate_slots[:, :, None] * hidden_slots.astype(jnp.float32)).astype(jnp.bfloat16)

    down_grad = lax.psum_scatter(
        jnp.einsum(
            "esd,esf->def", grad_slots, weighted, preferred_element_type=jnp.float32
        ).astype(jnp.bfloat16),
        "replica",
        scatter_dimension=0,
        tiled=True,
    )
    upstream = jnp.einsum(
        "esd,def->esf", grad_slots, down_weight, preferred_element_type=jnp.float32
    )
    hidden_grad = (gate_slots[:, :, None] * upstream).astype(jnp.bfloat16).reshape(hidden.shape)
    slot_grad = jnp.sum(hidden_slots.astype(jnp.float32) * upstream, axis=2)
    returned = lax.all_to_all(
        slot_grad.reshape(local_experts, expert_count, capacity),
        "expert",
        split_axis=1,
        concat_axis=1,
        tiled=True,
    )
    gate_grad = jnp.take(returned.reshape(-1), slot_index, axis=0)
    return (hidden_grad, down_grad, gate_grad)


def solution(mesh):
    in_specs = (
        P(("expert", "replica"), None),
        P(("expert", "replica"), None),
        P(("expert", "replica"), None),
        P("expert", "replica", None, None),
        P(None, "expert", None),
    )
    out_specs = (
        P("expert", "replica", None, None),
        P("replica", "expert", None),
        P(("expert", "replica"), None),
    )
    return jax.shard_map(
        per_device, mesh=mesh, in_specs=in_specs, out_specs=out_specs, check_vma=False
    )
```

```python
import jax
import jax.numpy as jnp
from jax import lax
from jax.experimental import pallas as pl
from jax.sharding import PartitionSpec as P


def pick_kernel(column_ref, rows_ref, out_ref):
    local, steps, block, width = out_ref.shape
    rows_per = column_ref.shape[1]
    group = rows_ref.shape[0] // steps
    tok = rows_ref.shape[1]
    for h in range(steps):
        column = column_ref[h]
        onehot = (
            column == lax.broadcasted_iota(jnp.int32, (rows_per, group * tok), 1)
        ).astype(rows_ref.dtype)
        rows = rows_ref[h * group:(h + 1) * group].reshape(group * tok, width)
        result = jnp.dot(onehot, rows, preferred_element_type=jnp.float32).astype(out_ref.dtype)
        for j in range(local):
            out_ref[j, h] = result[j * block:(j + 1) * block]


def pick(column, gathered, width, local):
    groups, rows_per, _ = column.shape
    sources, tok, _ = gathered.shape
    group = sources // groups
    block = rows_per // local
    steps = 2
    return pl.pallas_call(
        pick_kernel,
        out_shape=jax.ShapeDtypeStruct((local, groups, block, width), gathered.dtype),
        grid=(groups // steps,),
        in_specs=[
            pl.BlockSpec((steps, rows_per, 1), lambda g: (g, 0, 0)),
            pl.BlockSpec((steps * group, tok, width), lambda g: (g, 0, 0)),
        ],
        out_specs=pl.BlockSpec((local, steps, block, width), lambda g: (0, g, 0, 0)),
        cost_estimate=pl.CostEstimate(
            flops=2 * groups * rows_per * group * tok * width,
            bytes_accessed=sources * tok * width * 2 + groups * rows_per * width * 2,
            transcendentals=0,
        ),
    )(column, gathered)


def per_device(grad_out, gates, experts, hidden, down_weight):
    expert_count = lax.axis_size("expert")
    replica_count = lax.axis_size("replica")
    me = lax.axis_index("expert")
    tok_rows = grad_out.shape[0]
    width = grad_out.shape[1]
    top_count = experts.shape[1]
    local_experts = hidden.shape[0]
    slot_count = hidden.shape[2]
    hidden_width = hidden.shape[3]
    capacity = slot_count // expert_count
    all_experts = local_experts * expert_count

    flat_ids = experts.reshape(-1)
    expert_range = jnp.arange(all_experts, dtype=jnp.int32)
    onehot_ids = (flat_ids[:, None] == expert_range[None, :]).astype(jnp.int32)
    running = jnp.cumsum(onehot_ids, axis=0)
    position = jnp.sum(onehot_ids * running, axis=1) - 1
    slot_index = (
        flat_ids % local_experts * expert_count + flat_ids // local_experts
    ) * capacity + position
    slot_index = slot_index.reshape(tok_rows, top_count)

    info = jnp.concatenate([experts.astype(jnp.float32), gates.astype(jnp.float32)], axis=1)
    info = jnp.broadcast_to(info.reshape(1, -1), (expert_count, tok_rows * 2 * top_count))
    info = lax.all_to_all(info, "expert", split_axis=0, concat_axis=0, tiled=True)
    info = info.reshape(expert_count, tok_rows, 2 * top_count)
    all_ids = info[:, :, :top_count].astype(jnp.int32)
    all_gates = info[:, :, top_count:]
    gathered = lax.all_gather(grad_out, "expert")
    pair_ids = all_ids.reshape(expert_count, tok_rows * top_count).T
    local_ids = pair_ids - me * local_experts
    mine = local_ids[:, :, None] == jnp.arange(local_experts, dtype=jnp.int32)[None, None, :]
    mine = mine.reshape(tok_rows * top_count, expert_count * local_experts).astype(jnp.int32)
    rank = jnp.cumsum(mine, axis=0) - 1
    rank = jnp.where(mine > 0, rank, -1).reshape(
        tok_rows * top_count, expert_count, local_experts
    )
    hit = rank[..., None] == jnp.arange(capacity, dtype=jnp.int32)
    token_of = (jnp.arange(tok_rows * top_count, dtype=jnp.int32) // top_count + 1)
    owner = jnp.sum(jnp.where(hit, token_of[:, None, None, None], 0), axis=0) - 1
    gate_pairs = all_gates.reshape(expert_count, tok_rows * top_count).T
    gate_slots = jnp.sum(jnp.where(hit, gate_pairs[:, :, None, None], 0.0), axis=0)
    gate_slots = jnp.transpose(gate_slots, (1, 0, 2)).reshape(local_experts, slot_count)

    group = 4
    groups = expert_count // group
    within = (jnp.arange(expert_count, dtype=jnp.int32) % group * tok_rows)[:, None, None]
    column = jnp.where(owner >= 0, owner + within, -1)
    column = jnp.transpose(column.reshape(groups, group, local_experts, capacity), (0, 2, 1, 3))
    column = column.reshape(groups, local_experts * group * capacity, 1)
    grad_slots = pick(column, gathered, width, local_experts).reshape(
        local_experts, slot_count, width
    )

    hidden_slots = hidden.reshape(local_experts, slot_count, hidden_width)
    weighted = (gate_slots[:, :, None] * hidden_slots.astype(jnp.float32)).astype(jnp.bfloat16)

    down_grad = lax.psum_scatter(
        jnp.einsum(
            "esd,esf->def", grad_slots, weighted, preferred_element_type=jnp.float32
        ).astype(jnp.bfloat16),
        "replica",
        scatter_dimension=0,
        tiled=True,
    )
    upstream = jnp.einsum(
        "esd,def->esf", grad_slots, down_weight, preferred_element_type=jnp.float32
    )
    hidden_grad = (gate_slots[:, :, None] * upstream).astype(jnp.bfloat16).reshape(hidden.shape)
    slot_grad = jnp.sum(hidden_slots.astype(jnp.float32) * upstream, axis=2)
    returned = lax.all_to_all(
        slot_grad.reshape(local_experts, expert_count, capacity),
        "expert",
        split_axis=1,
        concat_axis=1,
        tiled=True,
    )
    gate_grad = jnp.take(returned.reshape(-1), slot_index, axis=0)
    return (hidden_grad, down_grad, gate_grad)


def solution(mesh):
    in_specs = (
        P(("expert", "replica"), None),
        P(("expert", "replica"), None),
        P(("expert", "replica"), None),
        P("expert", "replica", None, None),
        P(None, "expert", None),
    )
    out_specs = (
        P("expert", "replica", None, None),
        P("replica", "expert", None),
        P(("expert", "replica"), None),
    )
    return jax.shard_map(
        per_device, mesh=mesh, in_specs=in_specs, out_specs=out_specs, check_vma=False
    )
```

```python
import jax
import jax.numpy as jnp
from jax import lax
from jax.experimental import pallas as pl
from jax.sharding import PartitionSpec as P


def pick_kernel(column_ref, rows_ref, out_ref):
    local, steps, block, width = out_ref.shape
    rows_per = column_ref.shape[1]
    group = rows_ref.shape[0] // steps
    tok = rows_ref.shape[1]
    for h in range(steps):
        column = column_ref[h]
        onehot = (
            column == lax.broadcasted_iota(jnp.int32, (rows_per, group * tok), 1)
        ).astype(rows_ref.dtype)
        rows = rows_ref[h * group:(h + 1) * group].reshape(group * tok, width)
        result = jnp.dot(onehot, rows, preferred_element_type=jnp.float32).astype(out_ref.dtype)
        for j in range(local):
            out_ref[j, h] = result[j * block:(j + 1) * block]


def pick(column, gathered, width, local):
    groups, rows_per, _ = column.shape
    sources, tok, _ = gathered.shape
    group = sources // groups
    block = rows_per // local
    steps = 4
    return pl.pallas_call(
        pick_kernel,
        out_shape=jax.ShapeDtypeStruct((local, groups, block, width), gathered.dtype),
        grid=(groups // steps,),
        in_specs=[
            pl.BlockSpec((steps, rows_per, 1), lambda g: (g, 0, 0)),
            pl.BlockSpec((steps * group, tok, width), lambda g: (g, 0, 0)),
        ],
        out_specs=pl.BlockSpec((local, steps, block, width), lambda g: (0, g, 0, 0)),
        cost_estimate=pl.CostEstimate(
            flops=2 * groups * rows_per * group * tok * width,
            bytes_accessed=sources * tok * width * 2 + groups * rows_per * width * 2,
            transcendentals=0,
        ),
    )(column, gathered)


def per_device(grad_out, gates, experts, hidden, down_weight):
    expert_count = lax.axis_size("expert")
    replica_count = lax.axis_size("replica")
    me = lax.axis_index("expert")
    tok_rows = grad_out.shape[0]
    width = grad_out.shape[1]
    top_count = experts.shape[1]
    local_experts = hidden.shape[0]
    slot_count = hidden.shape[2]
    hidden_width = hidden.shape[3]
    capacity = slot_count // expert_count
    all_experts = local_experts * expert_count

    flat_ids = experts.reshape(-1)
    expert_range = jnp.arange(all_experts, dtype=jnp.int32)
    onehot_ids = (flat_ids[:, None] == expert_range[None, :]).astype(jnp.int32)
    running = jnp.cumsum(onehot_ids, axis=0)
    position = jnp.sum(onehot_ids * running, axis=1) - 1
    slot_index = (
        flat_ids % local_experts * expert_count + flat_ids // local_experts
    ) * capacity + position
    slot_index = slot_index.reshape(tok_rows, top_count)

    info = jnp.concatenate([experts.astype(jnp.float32), gates.astype(jnp.float32)], axis=1)
    info = jnp.broadcast_to(info.reshape(1, -1), (expert_count, tok_rows * 2 * top_count))
    info = lax.all_to_all(info, "expert", split_axis=0, concat_axis=0, tiled=True)
    info = info.reshape(expert_count, tok_rows, 2 * top_count)
    all_ids = info[:, :, :top_count].astype(jnp.int32)
    all_gates = info[:, :, top_count:]
    gathered = lax.all_gather(grad_out, "expert")
    pair_ids = all_ids.reshape(expert_count, tok_rows * top_count).T
    local_ids = pair_ids - me * local_experts
    mine = local_ids[:, :, None] == jnp.arange(local_experts, dtype=jnp.int32)[None, None, :]
    mine = mine.reshape(tok_rows * top_count, expert_count * local_experts).astype(jnp.int32)
    rank = jnp.cumsum(mine, axis=0) - 1
    rank = jnp.where(mine > 0, rank, -1).reshape(
        tok_rows * top_count, expert_count, local_experts
    )
    hit = rank[..., None] == jnp.arange(capacity, dtype=jnp.int32)
    token_of = (jnp.arange(tok_rows * top_count, dtype=jnp.int32) // top_count + 1)
    owner = jnp.sum(jnp.where(hit, token_of[:, None, None, None], 0), axis=0) - 1
    gate_pairs = all_gates.reshape(expert_count, tok_rows * top_count).T
    gate_slots = jnp.sum(jnp.where(hit, gate_pairs[:, :, None, None], 0.0), axis=0)
    gate_slots = jnp.transpose(gate_slots, (1, 0, 2)).reshape(local_experts, slot_count)

    group = 4
    groups = expert_count // group
    within = (jnp.arange(expert_count, dtype=jnp.int32) % group * tok_rows)[:, None, None]
    column = jnp.where(owner >= 0, owner + within, -1)
    column = jnp.transpose(column.reshape(groups, group, local_experts, capacity), (0, 2, 1, 3))
    column = column.reshape(groups, local_experts * group * capacity, 1)
    grad_slots = pick(column, gathered, width, local_experts).reshape(
        local_experts, slot_count, width
    )

    hidden_slots = hidden.reshape(local_experts, slot_count, hidden_width)
    weighted = (gate_slots[:, :, None] * hidden_slots.astype(jnp.float32)).astype(jnp.bfloat16)

    down_grad = lax.psum_scatter(
        jnp.einsum(
            "esd,esf->def", grad_slots, weighted, preferred_element_type=jnp.float32
        ).astype(jnp.bfloat16),
        "replica",
        scatter_dimension=0,
        tiled=True,
    )
    upstream = jnp.einsum(
        "esd,def->esf", grad_slots, down_weight, preferred_element_type=jnp.float32
    )
    hidden_grad = (gate_slots[:, :, None] * upstream).astype(jnp.bfloat16).reshape(hidden.shape)
    slot_grad = jnp.sum(hidden_slots.astype(jnp.float32) * upstream, axis=2)
    returned = lax.all_to_all(
        slot_grad.reshape(local_experts, expert_count, capacity),
        "expert",
        split_axis=1,
        concat_axis=1,
        tiled=True,
    )
    gate_grad = jnp.take(returned.reshape(-1), slot_index, axis=0)
    return (hidden_grad, down_grad, gate_grad)


def solution(mesh):
    in_specs = (
        P(("expert", "replica"), None),
        P(("expert", "replica"), None),
        P(("expert", "replica"), None),
        P("expert", "replica", None, None),
        P(None, "expert", None),
    )
    out_specs = (
        P("expert", "replica", None, None),
        P("replica", "expert", None),
        P(("expert", "replica"), None),
    )
    return jax.shard_map(
        per_device, mesh=mesh, in_specs=in_specs, out_specs=out_specs, check_vma=False
    )
```
